32 devices in a mesh: tx: 4 (over z), ty: 8 (over y, x, core).
Axes of the slice: x: 2, y: 2, z: 4, core: 2. Of those that a mesh axis runs over, the one named last changes fastest.
Arguments:
- frames: bfloat16 [4, 24, 1, 5, 384, 384], P('tx', 'ty'), may hold values from -6 to 6
- masks: int32 [4, 24, 12, 12], P('tx', 'ty'), may hold values 0 or 1
- phases: float32 [4, 24, 1], P('tx', 'ty'), may hold values from -3.140625 to 3.140625
- slot_tile: int32 [4, 24], P('tx', 'ty'), may hold values from -1 to 15, as said below
- otf: float32 [384, 384], replicated, may hold values from 0.05 to 1
- apod: float32 [384, 384], replicated, may hold values from 0.2 to 1
Outputs:
- stitched: float32 [2560, 2560], P('ty', 'tx')
The draws below stay inside these ranges and needn't reach their ends.
Inputs may be any that keep to these rules, and one draw needn't show every extreme that they name: `slot_tile`: in each column of devices, every tile is held in exactly one slot and is named 2 h + c for its tile row h and its tile column c within that column of devices; -1 marks an empty slot. The slots of one device never hold two tiles of the same tile row. In every draw some devices of every column hold 3 tiles.
All inputs are finite; a program needn't handle non-finite values. No bound on the sum of `masks` on one device may be relied on, other than what follows from the above.
Results may differ from the reference program's by a relative error of at most 0.0068.
Values may be sent and summed in bfloat16 or wider, within the bound.
A program may use at most 128 MiB of HBM per device.

```python
import math
import jax
import jax.numpy as jnp
from jax import lax

TILE_SIDE = 384
STRIDE = 320
ORIENT = 1
PHASES = 5
GROUP_COLS = 2
TILE_ROWS = 8
GROUPS = 4
SLOTS = 24
MASK_CELLS = 12
N_TY = 8


def shuffle_row(row_key):
    return jax.random.permutation(row_key, 3)


def group_table(group_key):
    first, second, third = jax.random.split(group_key, 3)
    worker_order = jax.random.permutation(first, TILE_ROWS)
    offset = 2 * jax.random.randint(second, (), 1, TILE_ROWS // 2)
    places = jnp.arange(TILE_ROWS, dtype=jnp.int32)
    start_row = (places - offset) % TILE_ROWS
    is_even = places % 2 == 0
    own_tile = 2 * places
    extra_one = jnp.where(is_even, 2 * start_row + 1, -1)
    extra_two = jnp.where(is_even, 2 * start_row + 3, -1)
    rows_by_place = jnp.stack([own_tile, extra_one, extra_two], axis=1)
    inverse = jnp.argsort(worker_order)
    slot_table = rows_by_place[inverse]
    row_keys = jax.random.split(third, TILE_ROWS)
    shuffle = jax.vmap(shuffle_row)(row_keys)
    slot_table = jnp.take_along_axis(slot_table, shuffle, axis=1)
    return slot_table.reshape(-1).astype(jnp.int32)


def draw_slot_tile(key, part):
    group_keys = jax.random.split(jax.random.fold_in(key, 17), GROUPS)
    return jax.vmap(group_table)(group_keys)


def with_ends(entries, key, low, top_value):
    shape = entries.shape
    index_at = [jax.random.randint(jax.random.fold_in(key, axis), (), 0, shape[axis]) for axis in range(len(shape))]
    entries = entries.at[tuple(index_at)].set(low)
    longest = shape.index(max(shape))
    index_at[longest] = (index_at[longest] + 1) % shape[longest]
    return entries.at[tuple(index_at)].set(top_value)


def block_levels(rng, dims, cuts, least, largest):
    def one(position, parts):
        draws = jax.random.uniform(jax.random.fold_in(jax.random.fold_in(rng, 6), position), (parts,), jnp.float32, least / len(cuts), largest / len(cuts))
        return jnp.repeat(jnp.exp(draws), dims[position] // parts).reshape((-1,) + (1,) * (len(dims) - position - 1))

    factor_of = one(*cuts[0])
    for cut in cuts[1:]:
        factor_of = factor_of * one(*cut)
    return factor_of


def normal_values(key, dims, spread, reach, shards=(), kind=jnp.bfloat16):
    drawn = spread * jax.random.normal(key, dims, jnp.float32)
    if shards:
        drawn = drawn * block_levels(key, dims, shards, -0.22, 0.18)
    return jnp.clip(drawn, -reach, reach).astype(kind)


def setup_inputs(seed: int = 0) -> dict:
    key_of = jax.random.split(jax.random.key(seed), 7)
    frames = normal_values(key_of[0], (GROUPS, SLOTS, ORIENT, PHASES, TILE_SIDE, TILE_SIDE), 1.0, 6.0, ((0, 4), (1, 8)))
    masks = with_ends((jax.random.randint(key_of[1], (GROUPS, SLOTS, MASK_CELLS, MASK_CELLS), 0, 4) < 3).astype(jnp.int32), jax.random.fold_in(key_of[1], 1), 0, 1)
    phases = jnp.clip(jax.random.uniform(key_of[2], (GROUPS, SLOTS, ORIENT), jnp.float32, -3.140625, 3.140625), -3.140625, 3.140625)
    slot_tile = draw_slot_tile(jax.random.fold_in(key_of[6], 71), 0)
    otf = jnp.clip(jnp.exp(jax.random.uniform(key_of[4], (TILE_SIDE, TILE_SIDE), jnp.float32, math.log(0.05), math.log(1.0))), 0.05, 1.0)
    apod = jnp.clip(jnp.exp(jax.random.uniform(key_of[5], (TILE_SIDE, TILE_SIDE), jnp.float32, math.log(0.2), math.log(1.0))), 0.2, 1.0)
    return dict(frames=frames, masks=masks, phases=phases, slot_tile=slot_tile, otf=otf, apod=apod)


wiener = 0.1
pattern_base = (37, 101)
pattern_step = (29, -53)


def batched(pattern, operand_a, operand_b):
    return jnp.einsum(pattern, operand_a.astype(jnp.float32), operand_b.astype(jnp.float32), precision=lax.Precision.HIGHEST)


def plain_dot(operand_a, operand_b):
    return jnp.dot(operand_a.astype(jnp.float32), operand_b.astype(jnp.float32), precision=lax.Precision.HIGHEST)


def mix_bands(pattern, operand_a, operand_b):
    return jnp.einsum(pattern, operand_a, operand_b, precision=lax.Precision.HIGHEST)


def dft_tables(length):
    places = jnp.arange(length, dtype=jnp.int32)
    product = (places[:, None] * places[None, :]) % length
    angles = product.astype(jnp.float32) * (2.0 * math.pi / length)
    return jnp.cos(angles).astype(jnp.bfloat16), jnp.sin(angles).astype(jnp.bfloat16)


def pattern_shift(orient):
    return (pattern_base[0] + orient * pattern_step[0], pattern_base[1] + orient * pattern_step[1])


def filter_weights(otf, apod, orient_count, phase_count):
    halfway = phase_count // 2
    rolled = []
    for orient in range(orient_count):
        shift_rows, shift_cols = pattern_shift(orient)
        for band_place in range(phase_count):
            band_order = band_place - halfway
            rolled.append(jnp.roll(otf, (-band_order * shift_rows, -band_order * shift_cols), (0, 1)))
    rolled_stack = jnp.stack(rolled)
    denominator = wiener + jnp.sum(rolled_stack * rolled_stack, axis=0)
    return rolled_stack * (apod / denominator)[None]


def tile_image(planes, cell_mask, offsets, gain_maps, cosine, sine_table):
    orient_count, phase_count, length = planes.shape[0], planes.shape[1], planes.shape[2]
    cell_count = cell_mask.shape[0]
    cell_width = length // cell_count
    shaped = planes.reshape(orient_count * phase_count, cell_count, cell_width, cell_count, cell_width)
    masked = (shaped * cell_mask.astype(jnp.bfloat16)[None, :, None, :, None]).reshape(orient_count * phase_count, length, length)
    first_real = batched("pjk,kl->pjl", masked, cosine).astype(jnp.bfloat16)
    first_imag = (-batched("pjk,kl->pjl", masked, sine_table)).astype(jnp.bfloat16)
    four_real = batched("jk,pkl->pjl", cosine, first_real) + batched("jk,pkl->pjl", sine_table, first_imag)
    four_imag = batched("jk,pkl->pjl", cosine, first_imag) - batched("jk,pkl->pjl", sine_table, first_real)
    halfway = phase_count // 2
    orders = jnp.arange(-halfway, halfway + 1).astype(jnp.float32)
    phase_steps = jnp.arange(phase_count).astype(jnp.float32) * (2.0 * math.pi / phase_count)
    spec_real = jnp.zeros((length, length), jnp.float32)
    spec_imag = jnp.zeros((length, length), jnp.float32)
    for orient in range(orient_count):
        shift_rows, shift_cols = pattern_shift(orient)
        angles = orders[:, None] * (offsets[orient] + phase_steps)[None, :]
        coef_real = jnp.cos(angles) / phase_count
        coef_imag = jnp.sin(angles) / phase_count
        part_real = four_real[orient * phase_count:(orient + 1) * phase_count]
        part_imag = four_imag[orient * phase_count:(orient + 1) * phase_count]
        band_real = mix_bands("mp,pxy->mxy", coef_real, part_real) + mix_bands("mp,pxy->mxy", coef_imag, part_imag)
        band_imag = mix_bands("mp,pxy->mxy", coef_real, part_imag) - mix_bands("mp,pxy->mxy", coef_imag, part_real)
        for band_place in range(phase_count):
            band_order = band_place - halfway
            offset_pair = (-band_order * shift_rows, -band_order * shift_cols)
            gain_map = gain_maps[orient * phase_count + band_place]
            spec_real = spec_real + gain_map * jnp.roll(band_real[band_place], offset_pair, (0, 1))
            spec_imag = spec_imag + gain_map * jnp.roll(band_imag[band_place], offset_pair, (0, 1))
    wave_real = spec_real.astype(jnp.bfloat16)
    wave_imag = spec_imag.astype(jnp.bfloat16)
    mid_real = (plain_dot(wave_real, cosine) - plain_dot(wave_imag, sine_table)).astype(jnp.bfloat16)
    mid_imag = (plain_dot(wave_real, sine_table) + plain_dot(wave_imag, cosine)).astype(jnp.bfloat16)
    return (plain_dot(cosine, mid_real) - plain_dot(sine_table, mid_imag)) * (1.0 / (length * length))


def ramp_weights(length, intersection, is_last):
    places = jnp.arange(length).astype(jnp.float32) + 0.5
    rising = jnp.minimum(places / intersection, 1.0)
    falling = jnp.minimum((length - places) / intersection, 1.0)
    return rising * jnp.where(is_last, jnp.ones_like(falling), falling)


def blended(picture, row_last, column_last, intersection):
    length = picture.shape[0]
    weighted = (picture * ramp_weights(length, intersection, row_last)[:, None]) * ramp_weights(length, intersection, column_last)[None, :]
    return weighted.astype(jnp.bfloat16)


def reference(frames, masks, phases, slot_tile, otf, apod):
    length = otf.shape[0]
    intersection = length - STRIDE
    group_count = frames.shape[0]
    row_count = N_TY
    tile_count = GROUP_COLS * row_count
    cosine, sine_table = dft_tables(length)
    gain_maps = filter_weights(otf, apod, frames.shape[2], frames.shape[3])
    slot_places = jnp.arange(frames.shape[1], dtype=jnp.int32)

    def locate(tile_list):
        target = jnp.where(tile_list >= 0, tile_list, tile_count).astype(jnp.int32)
        return jnp.zeros((tile_count,), jnp.int32).at[target].set(slot_places, mode="drop")

    slot_of = jax.vmap(locate)(slot_tile)
    canvas_full = jnp.zeros((STRIDE * row_count + intersection, STRIDE * GROUP_COLS * group_count + intersection), jnp.float32)

    def place_tile(number, canvas):
        group_id = (number // tile_count).astype(jnp.int32)
        tile_id = (number % tile_count).astype(jnp.int32)
        slot_id = slot_of[group_id, tile_id]
        picture = tile_image(frames[group_id, slot_id], masks[group_id, slot_id], phases[group_id, slot_id], gain_maps, cosine, sine_table)
        tile_row = tile_id // GROUP_COLS
        column = GROUP_COLS * group_id + tile_id % GROUP_COLS
        result = blended(picture, tile_row == row_count - 1, column == GROUP_COLS * group_count - 1, intersection)
        top_edge = (STRIDE * tile_row).astype(jnp.int32)
        left_edge = (STRIDE * column).astype(jnp.int32)
        region = lax.dynamic_slice(canvas, (top_edge, left_edge), (length, length))
        return lax.dynamic_update_slice(canvas, region + result.astype(jnp.float32), (top_edge, left_edge))

    canvas_full = lax.fori_loop(jnp.int32(0), jnp.int32(group_count * tile_count), place_tile, canvas_full)
    return canvas_full[intersection:, intersection:]
```

```python
import math

import jax
import jax.numpy as jnp
import numpy as np
from jax import lax
from jax.experimental import pallas as pl
from jax.experimental.pallas import tpu as pltpu
from jax.sharding import PartitionSpec as P

STRIDE = 320
GROUP_COLS = 2


wiener = 0.1
pattern_base = (37, 101)
pattern_step = (29, -53)


def passed_along(value, axis, steps):
    count = lax.axis_size(axis)
    leading, last = (max(0, -steps), min(count, count - steps))
    return lax.ppermute(value, axis, [(source, source + steps) for source in range(leading, last)])


def batched(pattern, operand_a, operand_b):
    return jnp.einsum(pattern, operand_a, operand_b, preferred_element_type=jnp.float32)


def pattern_shift(orient):
    return (pattern_base[0] + orient * pattern_step[0], pattern_base[1] + orient * pattern_step[1])


def tables(length, halfway):
    places = np.arange(length)
    angles = (places[:, None] * places[None, :] % length) * (2.0 * math.pi / length)
    cosine, sine = (np.cos(angles), np.sin(angles))
    rows, cols = pattern_shift(0)
    right, left = [], []
    for m in range(halfway + 1):
        right.append(np.concatenate([np.roll(cosine, -m * cols, 1), -np.roll(sine, -m * cols, 1)], 1))
        left.append(np.concatenate([np.roll(cosine, -m * rows, 0), np.roll(sine, -m * rows, 0)], 1))
    return (
        jnp.asarray(np.stack(right).astype(jnp.bfloat16)),
        jnp.asarray(np.stack(left).astype(jnp.bfloat16)),
    )


def dot(a, b):
    return jnp.dot(a, b, preferred_element_type=jnp.float32)


def tile_kernel(
    phase_count, cells, intersection,
    coef_ref, flags_ref, frames_ref, mask_ref, right_ref, left_ref, otf_ref, apod_ref,
    out_ref,
    wide_ref, gain_ref, images_ref, waves_ref, spec_ref, mid_ref,
):
    step = pl.program_id(0)
    length = otf_ref.shape[-1]
    halfway = phase_count // 2
    shift_rows, shift_cols = pattern_shift(0)
    chunk = length // 3

    @pl.when(step == 0)
    def _():
        for m in range(1, halfway + 1):
            c, neg_s = (right_ref[m, :, :length], right_ref[m, :, length:])
            wide_ref[m, :length, :length] = c
            wide_ref[m, :length, length:] = neg_s
            wide_ref[m, length:, :length] = -neg_s
            wide_ref[m, length:, length:] = c
        c, neg_s = (right_ref[0, :, :length], right_ref[0, :, length:])
        wide_ref[0, :length, :length] = c
        wide_ref[0, :length, length:] = -neg_s
        wide_ref[0, length:, :length] = neg_s
        wide_ref[0, length:, length:] = c

        for side in range(2):
            def rolled(m):
                value = otf_ref[side]
                if m == 0:
                    return value
                value = pltpu.roll(value, (-m * shift_rows) % length, 0)
                return pltpu.roll(value, (-m * shift_cols) % length, 1)

            total = jnp.full((length, length), wiener, jnp.float32)
            for m in range(-halfway, halfway + 1):
                value = rolled(m)
                total = total + value * value
                if side == 0 and m >= 0:
                    gain_ref[m] = value
                if side == 1 and m > 0:
                    spec_side = value
                    mid_slot = halfway + m
                    gain_ref[mid_slot] = spec_side
            scale = apod_ref[side] / total
            if side == 0:
                for m in range(halfway + 1):
                    gain_ref[m] = gain_ref[m] * scale
            else:
                for m in range(1, halfway + 1):
                    gain_ref[m] = gain_ref[m] + gain_ref[halfway + m] * scale

    width = length // cells
    for cell in range(cells):
        rows = pl.ds(cell * width, width)
        keep = mask_ref[0, cell:cell + 1, :].astype(jnp.float32)
        planes = [frames_ref[0, 0, 0, p, rows, :].astype(jnp.float32) * keep for p in range(phase_count)]
        total = planes[0]
        for p in range(1, phase_count):
            total = total + planes[p]
        images_ref[0, rows, :length] = (total * (1.0 / phase_count)).astype(jnp.bfloat16)
        for m in range(1, halfway + 1):
            for part in range(2):
                base = ((step * (halfway + 1) + m) * 2 + part) * phase_count
                total = planes[0] * coef_ref[base]
                for p in range(1, phase_count):
                    total = total + planes[p] * coef_ref[base + p]
                images_ref[m, rows, part * length:(part + 1) * length] = total.astype(jnp.bfloat16)

    for m in range(halfway + 1):
        for third in range(3):
            rows = pl.ds(third * chunk, chunk)
            lower = pl.ds(length + third * chunk, chunk)
            if m == 0:
                wave = dot(images_ref[0, rows, :length], right_ref[0])
            else:
                wave = dot(images_ref[m, rows, :], wide_ref[m])
            wave = wave.astype(jnp.bfloat16)
            waves_ref[m, rows, :] = wave
            waves_ref[m, lower, :length] = wave[:, length:]
            waves_ref[m, lower, length:] = -wave[:, :length]

    for third in range(3):
        rows = pl.ds(third * chunk, chunk)
        total = None
        for m in range(halfway + 1):
            band = dot(left_ref[m, rows, :], waves_ref[m])
            gain = gain_ref[m, rows, :]
            term = jnp.concatenate([gain, gain], axis=1) * band
            total = term if total is None else total + term
        spec_ref[rows, :] = total.astype(jnp.bfloat16)

    for third in range(3):
        rows = pl.ds(third * chunk, chunk)
        mid = dot(spec_ref[rows, :], wide_ref[0]).astype(jnp.bfloat16)
        mid_ref[rows, :] = mid[:, :length]
        mid_ref[pl.ds(length + third * chunk, chunk), :] = mid[:, length:]

    held = flags_ref[step * 3] > 0
    row_last = flags_ref[step * 3 + 1] > 0
    column_last = flags_ref[step * 3 + 2] > 0

    def ramp(places, is_last):
        places = places.astype(jnp.float32) + 0.5
        rising = jnp.minimum(places / intersection, 1.0)
        falling = jnp.minimum((length - places) / intersection, 1.0)
        return rising * jnp.where(is_last, jnp.ones_like(falling), falling)

    for third in range(3):
        rows = pl.ds(third * chunk, chunk)
        picture = dot(right_ref[0, rows, :], mid_ref[...]) * (1.0 / (length * length))
        places = lax.broadcasted_iota(jnp.int32, (chunk, length), 0) + third * chunk
        picture = picture * ramp(places, row_last)
        picture = picture * ramp(lax.broadcasted_iota(jnp.int32, (chunk, length), 1), column_last)
        out_ref[0, rows, :] = jnp.where(held, picture, 0.0).astype(jnp.bfloat16)


def reversed_map(value):
    return jnp.roll(value[::-1, ::-1], (1, 1), (0, 1))


def tile_results(frames, masks, phases, own_tiles, otf, apod, row_last, column_last, intersection):
    slot_count, phase_count = (frames.shape[1], frames.shape[3])
    length = otf.shape[0]
    cells = masks.shape[-1]
    halfway = phase_count // 2
    orders = jnp.arange(0, halfway + 1).astype(jnp.float32)
    phase_steps = jnp.arange(phase_count).astype(jnp.float32) * (2.0 * math.pi / phase_count)
    angles = orders[None, :, None] * (phases[0] + phase_steps[None, :])[:, None, :]
    coef = jnp.stack([jnp.cos(angles), -jnp.sin(angles)], axis=2) / phase_count
    flags = jnp.stack([own_tiles >= 0, row_last, column_last], axis=1).astype(jnp.int32)
    mask_rows = jnp.repeat(masks[0].astype(jnp.bfloat16), length // cells, axis=2)
    right, left = tables(length, halfway)
    otfs = jnp.stack([otf, reversed_map(otf)])
    apods = jnp.stack([apod, reversed_map(apod)])
    bands = halfway + 1

    def whole(array):
        return pl.BlockSpec(array.shape, lambda s: (0,) * array.ndim)

    return pl.pallas_call(
        lambda *refs: tile_kernel(phase_count, cells, intersection, *refs),
        grid=(slot_count,),
        in_specs=[
            pl.BlockSpec(memory_space=pltpu.SMEM),
            pl.BlockSpec(memory_space=pltpu.SMEM),
            pl.BlockSpec((1, 1) + frames.shape[2:], lambda s: (0, s, 0, 0, 0, 0)),
            pl.BlockSpec((1, cells, length), lambda s: (s, 0, 0)),
            whole(right), whole(left), whole(otfs), whole(apods),
        ],
        out_specs=pl.BlockSpec((1, length, length), lambda s: (s, 0, 0)),
        out_shape=jax.ShapeDtypeStruct((slot_count, length, length), jnp.bfloat16),
        scratch_shapes=[
            pltpu.VMEM((bands, 2 * length, 2 * length), jnp.bfloat16),
            pltpu.VMEM((2 * halfway + 1, length, length), jnp.float32),
            pltpu.VMEM((bands, length, 2 * length), jnp.bfloat16),
            pltpu.VMEM((bands, 2 * length, 2 * length), jnp.bfloat16),
            pltpu.VMEM((length, 2 * length), jnp.bfloat16),
            pltpu.VMEM((2 * length, length), jnp.bfloat16),
        ],
        compiler_params=pltpu.CompilerParams(vmem_limit_bytes=60 * 1024 * 1024),
    )(coef.reshape(-1), flags.reshape(-1), frames, mask_rows, right, left, otfs, apods)


def fold_rows(padded_block, intersection):
    arrived = passed_along(padded_block[:intersection].astype(jnp.bfloat16), "ty", -1).astype(
        jnp.float32
    )
    interior = padded_block[intersection:]
    keep_rows = interior.shape[0] - intersection
    return jnp.concatenate([interior[:keep_rows], interior[keep_rows:] + arrived], axis=0)


def fold_columns(padded_block, intersection):
    arrived = passed_along(padded_block[:, :intersection].astype(jnp.bfloat16), "tx", -1).astype(
        jnp.float32
    )
    interior = padded_block[:, intersection:]
    keep_cols = interior.shape[1] - intersection
    return jnp.concatenate([interior[:, :keep_cols], interior[:, keep_cols:] + arrived], axis=1)


def shards(frames, masks, phases, slot_tile, otf, apod):
    row_count = lax.axis_size("ty")
    group_count = lax.axis_size("tx")
    my_group = lax.axis_index("tx")
    length = otf.shape[0]
    intersection = length - STRIDE
    own_tiles = slot_tile[0]

    tile_rows = own_tiles // GROUP_COLS
    columns = GROUP_COLS * my_group + own_tiles % GROUP_COLS
    results = tile_results(
        frames, masks, phases, own_tiles, otf, apod,
        tile_rows == row_count - 1, columns == GROUP_COLS * group_count - 1, intersection,
    )
    column_places = jnp.arange(GROUP_COLS, dtype=jnp.int32)
    owner_rows = jnp.arange(row_count, dtype=jnp.int32)
    matches = ((own_tiles // GROUP_COLS)[:, None] == owner_rows[None, :]) & (own_tiles >= 0)[
        :, None
    ]
    choose = matches.astype(jnp.bfloat16)
    outgoing = batched("sh,sxy->hxy", choose, results).astype(jnp.bfloat16)
    labels = jnp.sum(matches.astype(jnp.int32) * (own_tiles % GROUP_COLS + 1)[:, None], axis=0) - 1
    incoming, column_tags = (
        lax.all_to_all(outgoing, "ty", split_axis=0, concat_axis=0, tiled=True),
        lax.all_to_all(labels[:, None], "ty", split_axis=0, concat_axis=0, tiled=True),
    )
    selector = (column_tags == column_places[None, :]).astype(jnp.bfloat16)
    tiles_here = batched("sc,sxy->cxy", selector, incoming)
    padded = jnp.zeros((length, STRIDE * GROUP_COLS + intersection), jnp.float32)
    for column_place in range(GROUP_COLS):
        padded = padded + jnp.pad(
            tiles_here[column_place],
            ((0, 0), (STRIDE * column_place, STRIDE * (GROUP_COLS - 1 - column_place))),
        )
    stitched = fold_columns(fold_rows(padded, intersection), intersection)
    return stitched


def solution(mesh):
    in_specs = (
        P("tx", "ty", None, None, None, None),
        P("tx", "ty", None, None),
        P("tx", "ty", None),
        P("tx", "ty"),
        P(),
        P(),
    )
    out_specs = P("ty", "tx")
    return jax.shard_map(shards, mesh=mesh, in_specs=in_specs, out_specs=out_specs, check_vma=False)
```

```python
import math

import jax
import jax.numpy as jnp
import numpy as np
from jax import lax
from jax.experimental import pallas as pl
from jax.experimental.pallas import tpu as pltpu
from jax.sharding import PartitionSpec as P

STRIDE = 320
GROUP_COLS = 2


wiener = 0.1
pattern_base = (37, 101)
pattern_step = (29, -53)


def pattern_shift(orient):
    return (pattern_base[0] + orient * pattern_step[0], pattern_base[1] + orient * pattern_step[1])


def tables(length, halfway):
    places = np.arange(length)
    angles = (places[:, None] * places[None, :] % length) * (2.0 * math.pi / length)
    cosine, sine = (np.cos(angles), np.sin(angles))
    rows, cols = pattern_shift(0)
    right, left = [], []
    for m in range(halfway + 1):
        right.append(np.concatenate([np.roll(cosine, -m * cols, 1), -np.roll(sine, -m * cols, 1)], 1))
        left.append(np.concatenate([np.roll(cosine, -m * rows, 0), np.roll(sine, -m * rows, 0)], 1))
    return (
        jnp.asarray(np.stack(right).astype(jnp.bfloat16)),
        jnp.asarray(np.stack(left).astype(jnp.bfloat16)),
    )


def dot(a, b):
    return jnp.dot(a, b, preferred_element_type=jnp.float32)


def tile_kernel(
    phase_count, cells, intersection, slot_count, bits,
    coef_ref, flags_ref, frames_ref, mask_ref, right_ref, left_ref, otf_ref, apod_ref, label_ref,
    out_ref,
    wide_ref, gain_ref, images_ref, waves_ref, spec_ref, mid_ref, tile_ref, twin_ref, cand_ref,
    names_ref, keep_ref, pack_ref, land_ref, hand_ref, final_ref, full_ref, up_ref, from_down_ref,
    from_right_ref, from_corner_ref, name_sems, twin_sems, cand_sems, pack_sems, final_sems, fold_sems,
):
    me = lax.axis_index("ty")
    count = lax.axis_size("ty")
    group = lax.axis_index("tx")
    groups = lax.axis_size("tx")
    half = lax.rem(me, 2)
    routes = (tuple(range(1, bits)), tuple(reversed(range(1, bits))))

    def across(mask):
        other = me
        for bit in range(bits):
            if mask >> bit & 1:
                other = other + (1 << bit) - 2 * (1 << bit) * lax.rem(me // (1 << bit), 2)
        return (group, other)

    up = lax.rem(me + count - 1, count)
    down = lax.rem(me + 1, count)
    before = lax.rem(group + groups - 1, groups)
    after = lax.rem(group + 1, groups)
    name_masks = [1] + [(1 << route[0]) | low for route in routes for low in (0, 1)]
    greeted = [across(mask) for mask in name_masks]
    greeted += [across(1 << bit) for bit in range(2, bits - 1)]
    greeted += [(group, up), (group, down), (before, me), (after, me), (before, up), (after, down)]

    def sent(src, dst, sems, index, target):
        return pltpu.make_async_remote_copy(
            src_ref=src, dst_ref=dst, send_sem=sems.at[(0,) + index], recv_sem=sems.at[(1,) + index],
            device_id=target, device_id_type=pl.DeviceIdType.MESH,
        )

    step = pl.program_id(0)
    length = otf_ref.shape[-1]
    halfway = phase_count // 2
    shift_rows, shift_cols = pattern_shift(0)
    chunk = length // 3
    part = length // 4
    own_rows = pl.multiple_of(half * (2 * part), 2 * part)
    twin_rows = pl.multiple_of((1 - half) * (2 * part), 2 * part)

    def name_copy(place):
        return sent(label_ref, names_ref.at[place], name_sems, (place,), across(name_masks[place]))

    def twin_copy(slot):
        return sent(tile_ref.at[slot, pl.ds(twin_rows, 2 * part)], twin_ref.at[slot], twin_sems, (slot,), across(1))

    def first_copy(slot, piece, who):
        if who == 0:
            src = tile_ref.at[slot, pl.ds(pl.multiple_of(own_rows + piece * part, part), part)]
        else:
            src = twin_ref.at[slot, pl.ds(piece * part, part)]
        return sent(src, cand_ref.at[piece, slot, who], cand_sems, (piece, slot, who), across(1 << routes[piece][0]))

    def relay(slot):
        twin_copy(slot).wait_recv()
        for piece in range(2):
            first_copy(slot, piece, 1).start()

    @pl.when(step == 0)
    def _():
        barrier = pltpu.get_barrier_semaphore()
        for target in greeted:
            pl.semaphore_signal(barrier, inc=1, device_id=target, device_id_type=pl.DeviceIdType.MESH)
        pl.semaphore_wait(barrier, len(greeted))
        for place in range(len(name_masks)):
            name_copy(place).start()

    @pl.when(step == 0)
    def _():
        for m in range(1, halfway + 1):
            c, neg_s = (right_ref[m, :, :length], right_ref[m, :, length:])
            wide_ref[m, :length, :length] = c
            wide_ref[m, :length, length:] = neg_s
            wide_ref[m, length:, :length] = -neg_s
            wide_ref[m, length:, length:] = c
        c, neg_s = (right_ref[0, :, :length], right_ref[0, :, length:])
        wide_ref[0, :length, :length] = c
        wide_ref[0, :length, length:] = -neg_s
        wide_ref[0, length:, :length] = neg_s
        wide_ref[0, length:, length:] = c

        for side in range(2):
            def rolled(m):
                value = otf_ref[side]
                if m == 0:
                    return value
                value = pltpu.roll(value, (-m * shift_rows) % length, 0)
                return pltpu.roll(value, (-m * shift_cols) % length, 1)

            total = jnp.full((length, length), wiener, jnp.float32)
            for m in range(-halfway, halfway + 1):
                value = rolled(m)
                total = total + value * value
                if side == 0 and m >= 0:
                    gain_ref[m] = value
                if side == 1 and m > 0:
                    spec_side = value
                    mid_slot = halfway + m
                    gain_ref[mid_slot] = spec_side
            scale = apod_ref[side] / total
            if side == 0:
                for m in range(halfway + 1):
                    gain_ref[m] = gain_ref[m] * scale
            else:
                for m in range(1, halfway + 1):
                    gain_ref[m] = gain_ref[m] + gain_ref[halfway + m] * scale

    width = length // cells
    for cell in range(cells):
        rows = pl.ds(cell * width, width)
        keep = mask_ref[0, cell:cell + 1, :].astype(jnp.float32)
        planes = [frames_ref[0, 0, 0, p, rows, :].astype(jnp.float32) * keep for p in range(phase_count)]
        total = planes[0]
        for p in range(1, phase_count):
            total = total + planes[p]
        images_ref[0, rows, :length] = (total * (1.0 / phase_count)).astype(jnp.bfloat16)
        for m in range(1, halfway + 1):
            for side in range(2):
                base = ((step * (halfway + 1) + m) * 2 + side) * phase_count
                total = planes[0] * coef_ref[base]
                for p in range(1, phase_count):
                    total = total + planes[p] * coef_ref[base + p]
                images_ref[m, rows, side * length:(side + 1) * length] = total.astype(jnp.bfloat16)

    @pl.when(step > 0)
    def _():
        relay(step - 1)

    for m in range(halfway + 1):
        for third in range(3):
            rows = pl.ds(third * chunk, chunk)
            lower = pl.ds(length + third * chunk, chunk)
            if m == 0:
                wave = dot(images_ref[0, rows, :length], right_ref[0])
            else:
                wave = dot(images_ref[m, rows, :], wide_ref[m])
            wave = wave.astype(jnp.bfloat16)
            waves_ref[m, rows, :] = wave
            waves_ref[m, lower, :length] = wave[:, length:]
            waves_ref[m, lower, length:] = -wave[:, :length]

    for third in range(3):
        rows = pl.ds(third * chunk, chunk)
        total = None
        for m in range(halfway + 1):
            band = dot(left_ref[m, rows, :], waves_ref[m])
            gain = gain_ref[m, rows, :]
            term = jnp.concatenate([gain, gain], axis=1) * band
            total = term if total is None else total + term
        spec_ref[rows, :] = total.astype(jnp.bfloat16)

    for third in range(3):
        rows = pl.ds(third * chunk, chunk)
        mid = dot(spec_ref[rows, :], wide_ref[0]).astype(jnp.bfloat16)
        mid_ref[rows, :] = mid[:, :length]
        mid_ref[pl.ds(length + third * chunk, chunk), :] = mid[:, length:]

    held = flags_ref[step * 3] > 0
    row_last = flags_ref[step * 3 + 1] > 0
    column_last = flags_ref[step * 3 + 2] > 0

    def ramp(places, is_last):
        places = places.astype(jnp.float32) + 0.5
        rising = jnp.minimum(places / intersection, 1.0)
        falling = jnp.minimum((length - places) / intersection, 1.0)
        return rising * jnp.where(is_last, jnp.ones_like(falling), falling)

    for third in range(3):
        rows = pl.ds(third * chunk, chunk)
        picture = dot(right_ref[0, rows, :], mid_ref[...]) * (1.0 / (length * length))
        places = lax.broadcasted_iota(jnp.int32, (chunk, length), 0) + third * chunk
        picture = picture * ramp(places, row_last)
        picture = picture * ramp(lax.broadcasted_iota(jnp.int32, (chunk, length), 1), column_last)
        tile_ref[step, rows, :] = jnp.where(held, picture, 0.0).astype(jnp.bfloat16)

    twin_copy(step).start()
    for piece in range(2):
        first_copy(step, piece, 0).start()

    @pl.when(step == slot_count - 1)
    def _():
        relay(slot_count - 1)
        for place in range(len(name_masks)):
            name_copy(place).wait()

        def candidate(piece, who, slot):
            if who == 0:
                return tile_ref[slot, pl.ds(pl.multiple_of(own_rows + piece * part, part), part), :]
            if who == 1:
                return twin_ref[slot, pl.ds(piece * part, part), :]
            return cand_ref[piece, slot, who - 2]

        def labels(piece, who, slot):
            if who == 0:
                return label_ref[slot:slot + 1, :]
            place = 0 if who == 1 else 1 + 2 * piece + (who - 2)
            return names_ref[place, slot:slot + 1, :]

        def combos(free):
            masks = [0]
            for bit in free:
                masks = masks + [mask | (1 << bit) for mask in masks]
            return masks

        def packed(piece, mask, column):
            wanted = across(mask)[1] * GROUP_COLS + column
            total = None
            for slot in range(slot_count):
                for who in range(4):
                    hit = jnp.where(labels(piece, who, slot) == wanted, 1.0, 0.0).astype(jnp.bfloat16)
                    term = candidate(piece, who, slot) * hit
                    total = term if total is None else total + term
            return total

        def pack_copy(piece, hop):
            size = GROUP_COLS << (len(routes[piece]) - hop)
            return sent(
                pack_ref.at[piece, hop - 1, pl.ds(0, size)], land_ref.at[piece, hop - 1, pl.ds(0, size)],
                pack_sems, (piece, hop - 1), across(1 << routes[piece][hop]),
            )

        for piece in range(2):
            for slot in range(slot_count):
                for who in range(2):
                    first_copy(slot, piece, who).wait_recv()
            route = routes[piece]
            rest = combos((0,) + route[2:])
            for place, mask in enumerate(rest):
                for column in range(GROUP_COLS):
                    pack_ref[piece, 0, place * GROUP_COLS + column] = packed(piece, mask | (1 << route[1]), column)
            pack_copy(piece, 1).start()
        for piece in range(2):
            for place, mask in enumerate(combos((0,) + routes[piece][2:])):
                for column in range(GROUP_COLS):
                    keep_ref[piece, place * GROUP_COLS + column] = packed(piece, mask, column)
        for hop in range(1, bits - 1):
            for piece in range(2):
                pack_copy(piece, hop).wait_recv()
                size = GROUP_COLS << (bits - 1 - hop)
                if hop < bits - 2:
                    held_order = combos((0,) + routes[piece][hop + 1:])
                    later = combos((0,) + routes[piece][hop + 2:])
                    bit = 1 << routes[piece][hop + 1]
                    for place, mask in enumerate(later):
                        there = held_order.index(mask | bit)
                        here = held_order.index(mask)
                        for column in range(GROUP_COLS):
                            i, j, k = (there * GROUP_COLS + column, here * GROUP_COLS + column, place * GROUP_COLS + column)
                            pack_ref[piece, hop, k] = keep_ref[piece, i] + land_ref[piece, hop - 1, i]
                            keep_ref[piece, k] = keep_ref[piece, j] + land_ref[piece, hop - 1, j]
                    pack_copy(piece, hop + 1).start()
                else:
                    for column in range(GROUP_COLS):
                        hand_ref[piece, column] = keep_ref[piece, GROUP_COLS + column] + land_ref[piece, hop - 1, GROUP_COLS + column]
                    sent(hand_ref.at[piece], final_ref.at[piece], final_sems, (piece,), across(1)).start()
        for piece in range(2):
            rows = pl.ds(pl.multiple_of(own_rows + piece * part, part), part)
            for column in range(GROUP_COLS):
                full_ref[column, rows, :] = keep_ref[piece, column] + land_ref[piece, bits - 3, column]
        for piece in range(2):
            sent(hand_ref.at[piece], final_ref.at[piece], final_sems, (piece,), across(1)).wait_recv()
            rows = pl.ds(pl.multiple_of(twin_rows + piece * part, part), part)
            for column in range(GROUP_COLS):
                full_ref[column, rows, :] = final_ref[piece, column]

        side = 2 * intersection
        inner = length - intersection
        top = pl.ds(0, intersection)
        low = pl.ds(intersection, inner)

        fold_left = sent(full_ref.at[0, low, pl.ds(0, side)], from_right_ref, fold_sems, (0,), (before, me))
        fold_corner = sent(full_ref.at[0, top, pl.ds(0, side)], from_corner_ref, fold_sems, (1,), (before, up))
        fold_up = sent(up_ref, from_down_ref, fold_sems, (2,), (group, up))
        fold_left.start()
        fold_corner.start()

        def panel(rows, size):
            total = None
            for column in range(GROUP_COLS):
                value = full_ref[column, rows, :].astype(jnp.float32)
                start = STRIDE * column - intersection
                if start < 0:
                    value = value[:, -start:]
                    start = 0
                ends = [jnp.zeros((size, start), jnp.float32), value]
                ends.append(jnp.zeros((size, STRIDE * GROUP_COLS - start - value.shape[1]), jnp.float32))
                value = jnp.concatenate([piece for piece in ends if piece.shape[1]], axis=1)
                total = value if total is None else total + value
            return total

        up_ref[...] = panel(top, intersection).astype(jnp.bfloat16)
        fold_up.start()
        out_ref[...] = panel(low, inner)
        wide = STRIDE * GROUP_COLS
        not_low = jnp.where(me < count - 1, 1.0, 0.0)
        not_right = jnp.where(group < groups - 1, 1.0, 0.0)
        tail_rows = pl.ds(inner - intersection, intersection)

        def at_right(value):
            return jnp.concatenate([jnp.zeros((value.shape[0], side - intersection), jnp.float32), value[:, :intersection].astype(jnp.float32)], axis=1)

        fold_left.wait_recv()
        out_ref[:, wide - side:] = out_ref[:, wide - side:] + at_right(from_right_ref[...]) * not_right
        fold_up.wait_recv()
        out_ref[tail_rows, :] = out_ref[tail_rows, :] + from_down_ref[...].astype(jnp.float32) * not_low
        fold_corner.wait_recv()
        out_ref[tail_rows, wide - side:] = out_ref[tail_rows, wide - side:] + at_right(from_corner_ref[...]) * (not_right * not_low)

        for slot in range(slot_count):
            twin_copy(slot).wait_send()
            for piece in range(2):
                for who in range(2):
                    first_copy(slot, piece, who).wait_send()
        for piece in range(2):
            for hop in range(1, bits - 1):
                pack_copy(piece, hop).wait_send()
            sent(hand_ref.at[piece], final_ref.at[piece], final_sems, (piece,), across(1)).wait_send()
        fold_left.wait_send()
        fold_corner.wait_send()
        fold_up.wait_send()


def reversed_map(value):
    return jnp.roll(value[::-1, ::-1], (1, 1), (0, 1))


def stitched_block(frames, masks, phases, own_tiles, otf, apod, row_last, column_last, intersection):
    slot_count, phase_count = (frames.shape[1], frames.shape[3])
    length = otf.shape[0]
    cells = masks.shape[-1]
    halfway = phase_count // 2
    orders = jnp.arange(0, halfway + 1).astype(jnp.float32)
    phase_steps = jnp.arange(phase_count).astype(jnp.float32) * (2.0 * math.pi / phase_count)
    angles = orders[None, :, None] * (phases[0] + phase_steps[None, :])[:, None, :]
    coef = jnp.stack([jnp.cos(angles), -jnp.sin(angles)], axis=2) / phase_count
    flags = jnp.stack([own_tiles >= 0, row_last, column_last], axis=1).astype(jnp.int32)
    mask_rows = jnp.repeat(masks[0].astype(jnp.bfloat16), length // cells, axis=2)
    right, left = tables(length, halfway)
    otfs = jnp.stack([otf, reversed_map(otf)])
    apods = jnp.stack([apod, reversed_map(apod)])
    bands = halfway + 1
    count = lax.axis_size("ty")
    bits = count.bit_length() - 1
    part = length // 4
    wide = STRIDE * GROUP_COLS
    slot_rows = -(-slot_count // 8) * 8
    names = jnp.broadcast_to(jnp.pad(own_tiles, (0, slot_rows - slot_count), constant_values=-1)[:, None], (slot_rows, length))
    most = GROUP_COLS << (bits - 2)
    dma = pltpu.SemaphoreType.DMA

    def whole(array):
        return pl.BlockSpec(array.shape, lambda s: (0,) * array.ndim)

    return pl.pallas_call(
        lambda *refs: tile_kernel(phase_count, cells, intersection, slot_count, bits, *refs),
        grid=(slot_count,),
        in_specs=[
            pl.BlockSpec(memory_space=pltpu.SMEM),
            pl.BlockSpec(memory_space=pltpu.SMEM),
            pl.BlockSpec((1, 1) + frames.shape[2:], lambda s: (0, s, 0, 0, 0, 0)),
            pl.BlockSpec((1, cells, length), lambda s: (s, 0, 0)),
            whole(right), whole(left), whole(otfs), whole(apods), whole(names),
        ],
        out_specs=pl.BlockSpec((STRIDE, wide), lambda s: (0, 0)),
        out_shape=jax.ShapeDtypeStruct((STRIDE, wide), jnp.float32),
        scratch_shapes=[
            pltpu.VMEM((bands, 2 * length, 2 * length), jnp.bfloat16),
            pltpu.VMEM((2 * halfway + 1, length, length), jnp.float32),
            pltpu.VMEM((bands, length, 2 * length), jnp.bfloat16),
            pltpu.VMEM((bands, 2 * length, 2 * length), jnp.bfloat16),
            pltpu.VMEM((length, 2 * length), jnp.bfloat16),
            pltpu.VMEM((2 * length, length), jnp.bfloat16),
            pltpu.VMEM((slot_count, length, length), jnp.bfloat16),
            pltpu.VMEM((slot_count, 2 * part, length), jnp.bfloat16),
            pltpu.VMEM((2, slot_count, 2, part, length), jnp.bfloat16),
            pltpu.VMEM((5, slot_rows, length), jnp.int32),
            pltpu.VMEM((2, most, part, length), jnp.bfloat16),
            pltpu.VMEM((2, bits - 2, most, part, length), jnp.bfloat16),
            pltpu.VMEM((2, bits - 2, most, part, length), jnp.bfloat16),
            pltpu.VMEM((2, GROUP_COLS, part, length), jnp.bfloat16),
            pltpu.VMEM((2, GROUP_COLS, part, length), jnp.bfloat16),
            pltpu.VMEM((GROUP_COLS, length, length), jnp.bfloat16),
            pltpu.VMEM((intersection, wide), jnp.bfloat16),
            pltpu.VMEM((intersection, wide), jnp.bfloat16),
            pltpu.VMEM((length - intersection, 2 * intersection), jnp.bfloat16),
            pltpu.VMEM((intersection, 2 * intersection), jnp.bfloat16),
            dma((2, 5)),
            dma((2, slot_count)),
            dma((2, 2, slot_count, 2)),
            dma((2, 2, bits - 2)),
            dma((2, 2)),
            dma((2, 3)),
        ],
        compiler_params=pltpu.CompilerParams(
            vmem_limit_bytes=60 * 1024 * 1024, collective_id=0, has_side_effects=True
        ),
    )(coef.reshape(-1), flags.reshape(-1), frames, mask_rows, right, left, otfs, apods, names)


def shards(frames, masks, phases, slot_tile, otf, apod):
    row_count = lax.axis_size("ty")
    group_count = lax.axis_size("tx")
    my_group = lax.axis_index("tx")
    length = otf.shape[0]
    intersection = length - STRIDE
    own_tiles = slot_tile[0]

    tile_rows = own_tiles // GROUP_COLS
    columns = GROUP_COLS * my_group + own_tiles % GROUP_COLS
    return stitched_block(
        frames, masks, phases, own_tiles, otf, apod,
        tile_rows == row_count - 1, columns == GROUP_COLS * group_count - 1, intersection,
    )


def solution(mesh):
    in_specs = (
        P("tx", "ty", None, None, None, None),
        P("tx", "ty", None, None),
        P("tx", "ty", None),
        P("tx", "ty"),
        P(),
        P(),
    )
    out_specs = P("ty", "tx")
    return jax.shard_map(shards, mesh=mesh, in_specs=in_specs, out_specs=out_specs, check_vma=False)
```

```python
import math

import jax
import jax.numpy as jnp
import numpy as np
from jax import lax
from jax.experimental import pallas as pl
from jax.experimental.pallas import tpu as pltpu
from jax.sharding import PartitionSpec as P

STRIDE = 320
GROUP_COLS = 2


wiener = 0.1
pattern_base = (37, 101)
pattern_step = (29, -53)


def pattern_shift(orient):
    return (pattern_base[0] + orient * pattern_step[0], pattern_base[1] + orient * pattern_step[1])


def tables(length, halfway):
    places = np.arange(length)
    angles = (places[:, None] * places[None, :] % length) * (2.0 * math.pi / length)
    cosine, sine = (np.cos(angles), np.sin(angles))
    rows, cols = pattern_shift(0)
    right, left = [], []
    for m in range(halfway + 1):
        right.append(np.concatenate([np.roll(cosine, -m * cols, 1), -np.roll(sine, -m * cols, 1)], 1))
        left.append(np.concatenate([np.roll(cosine, -m * rows, 0), np.roll(sine, -m * rows, 0)], 1))
    return (
        jnp.asarray(np.stack(right).astype(jnp.bfloat16)),
        jnp.asarray(np.stack(left[1:]).astype(jnp.bfloat16)),
    )


def dot(a, b):
    return jnp.dot(a, b, preferred_element_type=jnp.float32)


def tile_kernel(
    phase_count, cells, intersection, slot_count, bits,
    phase_ref, tiles_ref, frames_ref, mask_ref, right_ref, left_ref, otf_ref, apod_ref,
    out_ref,
    label_ref, flip_ref, left0_ref, wide_ref, gain_ref, images_ref, waves_ref, spec_ref, mid_ref, tile_ref, twin_ref, cand_ref,
    names_ref, keep_ref, pack_ref, land_ref, hand_ref, final_ref, full_ref, up_ref, from_down_ref,
    from_right_ref, from_corner_ref, name_sems, twin_sems, cand_sems, pack_sems, final_sems, fold_sems,
):
    me = lax.axis_index("ty")
    count = lax.axis_size("ty")
    group = lax.axis_index("tx")
    groups = lax.axis_size("tx")
    half = lax.rem(me, 2)
    routes = (tuple(range(1, bits)), tuple(reversed(range(1, bits))))

    def across(mask):
        other = me
        for bit in range(bits):
            if mask >> bit & 1:
                other = other + (1 << bit) - 2 * (1 << bit) * lax.rem(me // (1 << bit), 2)
        return (group, other)

    up = lax.rem(me + count - 1, count)
    down = lax.rem(me + 1, count)
    before = lax.rem(group + groups - 1, groups)
    after = lax.rem(group + 1, groups)
    name_masks = [1] + [(1 << route[0]) | low for route in routes for low in (0, 1)]
    greeted = [across(mask) for mask in name_masks]
    greeted += [across(1 << bit) for bit in range(2, bits - 1)]
    greeted += [(group, up), (group, down), (before, me), (after, me), (before, up), (after, down)]

    def sent(src, dst, sems, index, target):
        return pltpu.make_async_remote_copy(
            src_ref=src, dst_ref=dst, send_sem=sems.at[(0,) + index], recv_sem=sems.at[(1,) + index],
            device_id=target, device_id_type=pl.DeviceIdType.MESH,
        )

    step = pl.program_id(0)
    length = otf_ref.shape[-1]
    halfway = phase_count // 2
    shift_rows, shift_cols = pattern_shift(0)
    chunk = length // 3
    part = length // 4
    own_rows = pl.multiple_of(half * (2 * part), 2 * part)
    twin_rows = pl.multiple_of((1 - half) * (2 * part), 2 * part)

    def name_copy(place):
        return sent(label_ref, names_ref.at[place], name_sems, (place,), across(name_masks[place]))

    def twin_copy(slot):
        return sent(tile_ref.at[slot, pl.ds(twin_rows, 2 * part)], twin_ref.at[slot], twin_sems, (slot,), across(1))

    def first_copy(slot, piece, who):
        if who == 0:
            src = tile_ref.at[slot, pl.ds(pl.multiple_of(own_rows + piece * part, part), part)]
        else:
            src = twin_ref.at[slot, pl.ds(piece * part, part)]
        return sent(src, cand_ref.at[piece, slot, who], cand_sems, (piece, slot, who), across(1 << routes[piece][0]))

    def relay(slot):
        twin_copy(slot).wait_recv()
        for piece in range(2):
            first_copy(slot, piece, 1).start()

    @pl.when(step == 0)
    def _():
        barrier = pltpu.get_barrier_semaphore()
        for target in greeted:
            pl.semaphore_signal(barrier, inc=1, device_id=target, device_id_type=pl.DeviceIdType.MESH)
        pl.semaphore_wait(barrier, len(greeted))
        label_ref[...] = jnp.full(label_ref.shape, -1, jnp.int32)
        for slot in range(slot_count):
            label_ref[slot:slot + 1, :] = jnp.full((1, length), tiles_ref[slot], jnp.int32)
        for place in range(len(name_masks)):
            name_copy(place).start()

    @pl.when(step == 0)
    def _():
        for m in range(1, halfway + 1):
            c, neg_s = (right_ref[m, :, :length], right_ref[m, :, length:])
            wide_ref[m, :length, :length] = c
            wide_ref[m, :length, length:] = neg_s
            wide_ref[m, length:, :length] = -neg_s
            wide_ref[m, length:, length:] = c
        c, neg_s = (right_ref[0, :, :length], right_ref[0, :, length:])
        wide_ref[0, :length, :length] = c
        wide_ref[0, :length, length:] = -neg_s
        wide_ref[0, length:, :length] = neg_s
        wide_ref[0, length:, length:] = c
        left0_ref[:, :length] = c
        left0_ref[:, length:] = -neg_s

        index_sum = lax.broadcasted_iota(jnp.int32, (length, length), 0) + lax.broadcasted_iota(jnp.int32, (length, length), 1)
        swap = jnp.where((index_sum == 0) | (index_sum == length), 1.0, 0.0).astype(jnp.bfloat16)
        for place, source in enumerate((otf_ref, apod_ref)):
            value = source[...]
            high = value.astype(jnp.bfloat16)
            rest = (value - high.astype(jnp.float32)).astype(jnp.bfloat16)
            turned = None
            for piece in (high, rest):
                term = dot(dot(swap, piece).astype(jnp.bfloat16), swap)
                turned = term if turned is None else turned + term
            flip_ref[place] = turned

        for side in range(2):
            def rolled(m):
                value = otf_ref[...] if side == 0 else flip_ref[0]
                if m == 0:
                    return value
                value = pltpu.roll(value, (-m * shift_rows) % length, 0)
                return pltpu.roll(value, (-m * shift_cols) % length, 1)

            total = jnp.full((length, length), wiener, jnp.float32)
            for m in range(-halfway, halfway + 1):
                value = rolled(m)
                total = total + value * value
                if side == 0 and m >= 0:
                    gain_ref[m] = value
                if side == 1 and m > 0:
                    spec_side = value
                    mid_slot = halfway + m
                    gain_ref[mid_slot] = spec_side
            scale = (apod_ref[...] if side == 0 else flip_ref[1]) / total
            if side == 0:
                for m in range(halfway + 1):
                    gain_ref[m] = gain_ref[m] * scale
            else:
                for m in range(1, halfway + 1):
                    gain_ref[m] = gain_ref[m] + gain_ref[halfway + m] * scale

    width = length // cells
    spread = jnp.where(
        lax.broadcasted_iota(jnp.int32, (cells, length), 1) // width
        == lax.broadcasted_iota(jnp.int32, (cells, length), 0), 1.0, 0.0).astype(jnp.bfloat16)
    mask_rows = dot(mask_ref[0, 0].astype(jnp.float32).astype(jnp.bfloat16), spread)
    places = (lax.broadcasted_iota(jnp.int32, (8, 128), 0), lax.broadcasted_iota(jnp.int32, (8, 128), 1))
    angles = places[0].astype(jnp.float32) * (
        phase_ref[step] + places[1].astype(jnp.float32) * (2.0 * math.pi / phase_count))
    coefs = (jnp.cos(angles) / phase_count, -jnp.sin(angles) / phase_count)
    weights = [[[jnp.broadcast_to(coefs[side][m:m + 1, p:p + 1], (width, length)) for p in range(phase_count)]
                for side in range(2)] for m in range(1, halfway + 1)]
    for cell in range(cells):
        rows = pl.ds(cell * width, width)
        keep = mask_rows[cell:cell + 1, :]
        planes = [frames_ref[0, 0, 0, p, rows, :].astype(jnp.float32) * keep for p in range(phase_count)]
        total = planes[0]
        for p in range(1, phase_count):
            total = total + planes[p]
        images_ref[0, rows, :length] = (total * (1.0 / phase_count)).astype(jnp.bfloat16)
        for m in range(1, halfway + 1):
            for side in range(2):
                weight = weights[m - 1][side]
                total = planes[0] * weight[0]
                for p in range(1, phase_count):
                    total = total + planes[p] * weight[p]
                images_ref[m, rows, side * length:(side + 1) * length] = total.astype(jnp.bfloat16)

    @pl.when(step > 0)
    def _():
        relay(step - 1)

    for m in range(halfway + 1):
        for third in range(3):
            rows = pl.ds(third * chunk, chunk)
            lower = pl.ds(length + third * chunk, chunk)
            if m == 0:
                wave = dot(images_ref[0, rows, :length], right_ref[0])
            else:
                wave = dot(images_ref[m, rows, :], wide_ref[m])
            wave = wave.astype(jnp.bfloat16)
            waves_ref[m, rows, :] = wave
            waves_ref[m, lower, :length] = wave[:, length:]
            waves_ref[m, lower, length:] = -wave[:, :length]

    for third in range(3):
        rows = pl.ds(third * chunk, chunk)
        total = None
        for m in range(halfway + 1):
            band = dot(left_ref[m - 1, rows, :] if m else left0_ref[rows, :], waves_ref[m])
            gain = gain_ref[m, rows, :]
            term = jnp.concatenate([gain, gain], axis=1) * band
            total = term if total is None else total + term
        spec_ref[rows, :] = total.astype(jnp.bfloat16)

    for third in range(3):
        rows = pl.ds(third * chunk, chunk)
        mid = dot(spec_ref[rows, :], wide_ref[0]).astype(jnp.bfloat16)
        mid_ref[rows, :] = mid[:, :length]
        mid_ref[pl.ds(length + third * chunk, chunk), :] = mid[:, length:]

    tile = tiles_ref[step]
    held = tile >= 0
    row_last = tile >= (count - 1) * GROUP_COLS
    column_last = lax.rem(jnp.maximum(tile, 0), GROUP_COLS) + GROUP_COLS * group == GROUP_COLS * groups - 1

    def ramp(places, is_last):
        places = places.astype(jnp.float32) + 0.5
        rising = jnp.minimum(places / intersection, 1.0)
        falling = jnp.minimum((length - places) / intersection, 1.0)
        return rising * jnp.where(is_last, jnp.ones_like(falling), falling)

    for third in range(3):
        rows = pl.ds(third * chunk, chunk)
        picture = dot(right_ref[0, rows, :], mid_ref[...]) * (1.0 / (length * length))
        places = lax.broadcasted_iota(jnp.int32, (chunk, length), 0) + third * chunk
        picture = picture * ramp(places, row_last)
        picture = picture * ramp(lax.broadcasted_iota(jnp.int32, (chunk, length), 1), column_last)
        tile_ref[step, rows, :] = jnp.where(held, picture, 0.0).astype(jnp.bfloat16)

    twin_copy(step).start()
    for piece in range(2):
        first_copy(step, piece, 0).start()

    @pl.when(step == slot_count - 1)
    def _():
        relay(slot_count - 1)
        for place in range(len(name_masks)):
            name_copy(place).wait()

        def candidate(piece, who, slot):
            if who == 0:
                return tile_ref[slot, pl.ds(pl.multiple_of(own_rows + piece * part, part), part), :]
            if who == 1:
                return twin_ref[slot, pl.ds(piece * part, part), :]
            return cand_ref[piece, slot, who - 2]

        def labels(piece, who, slot):
            if who == 0:
                return label_ref[slot:slot + 1, :]
            place = 0 if who == 1 else 1 + 2 * piece + (who - 2)
            return names_ref[place, slot:slot + 1, :]

        def combos(free):
            masks = [0]
            for bit in free:
                masks = masks + [mask | (1 << bit) for mask in masks]
            return masks

        def packed(piece, mask, column):
            wanted = across(mask)[1] * GROUP_COLS + column
            total = None
            for slot in range(slot_count):
                for who in range(4):
                    hit = jnp.where(labels(piece, who, slot) == wanted, 1.0, 0.0).astype(jnp.bfloat16)
                    term = candidate(piece, who, slot) * hit
                    total = term if total is None else total + term
            return total

        def pack_copy(piece, hop):
            size = GROUP_COLS << (len(routes[piece]) - hop)
            return sent(
                pack_ref.at[piece, hop - 1, pl.ds(0, size)], land_ref.at[piece, hop - 1, pl.ds(0, size)],
                pack_sems, (piece, hop - 1), across(1 << routes[piece][hop]),
            )

        for piece in range(2):
            for slot in range(slot_count):
                for who in range(2):
                    first_copy(slot, piece, who).wait_recv()
            route = routes[piece]
            rest = combos((0,) + route[2:])
            for place, mask in enumerate(rest):
                for column in range(GROUP_COLS):
                    pack_ref[piece, 0, place * GROUP_COLS + column] = packed(piece, mask | (1 << route[1]), column)
            pack_copy(piece, 1).start()
        for piece in range(2):
            for place, mask in enumerate(combos((0,) + routes[piece][2:])):
                for column in range(GROUP_COLS):
                    keep_ref[piece, place * GROUP_COLS + column] = packed(piece, mask, column)
        for hop in range(1, bits - 1):
            for piece in range(2):
                pack_copy(piece, hop).wait_recv()
                size = GROUP_COLS << (bits - 1 - hop)
                if hop < bits - 2:
                    held_order = combos((0,) + routes[piece][hop + 1:])
                    later = combos((0,) + routes[piece][hop + 2:])
                    bit = 1 << routes[piece][hop + 1]
                    for place, mask in enumerate(later):
                        there = held_order.index(mask | bit)
                        here = held_order.index(mask)
                        for column in range(GROUP_COLS):
                            i, j, k = (there * GROUP_COLS + column, here * GROUP_COLS + column, place * GROUP_COLS + column)
                            pack_ref[piece, hop, k] = keep_ref[piece, i] + land_ref[piece, hop - 1, i]
                            keep_ref[piece, k] = keep_ref[piece, j] + land_ref[piece, hop - 1, j]
                    pack_copy(piece, hop + 1).start()
                else:
                    for column in range(GROUP_COLS):
                        hand_ref[piece, column] = keep_ref[piece, GROUP_COLS + column] + land_ref[piece, hop - 1, GROUP_COLS + column]
                    sent(hand_ref.at[piece], final_ref.at[piece], final_sems, (piece,), across(1)).start()
        for piece in range(2):
            rows = pl.ds(pl.multiple_of(own_rows + piece * part, part), part)
            for column in range(GROUP_COLS):
                full_ref[column, rows, :] = keep_ref[piece, column] + land_ref[piece, bits - 3, column]
        for piece in range(2):
            sent(hand_ref.at[piece], final_ref.at[piece], final_sems, (piece,), across(1)).wait_recv()
            rows = pl.ds(pl.multiple_of(twin_rows + piece * part, part), part)
            for column in range(GROUP_COLS):
                full_ref[column, rows, :] = final_ref[piece, column]

        side = 2 * intersection
        inner = length - intersection
        top = pl.ds(0, intersection)
        low = pl.ds(intersection, inner)

        fold_left = sent(full_ref.at[0, low, pl.ds(0, side)], from_right_ref, fold_sems, (0,), (before, me))
        fold_corner = sent(full_ref.at[0, top, pl.ds(0, side)], from_corner_ref, fold_sems, (1,), (before, up))
        fold_up = sent(up_ref, from_down_ref, fold_sems, (2,), (group, up))
        fold_left.start()
        fold_corner.start()

        def panel(rows, size):
            total = None
            for column in range(GROUP_COLS):
                value = full_ref[column, rows, :].astype(jnp.float32)
                start = STRIDE * column - intersection
                if start < 0:
                    value = value[:, -start:]
                    start = 0
                ends = [jnp.zeros((size, start), jnp.float32), value]
                ends.append(jnp.zeros((size, STRIDE * GROUP_COLS - start - value.shape[1]), jnp.float32))
                value = jnp.concatenate([piece for piece in ends if piece.shape[1]], axis=1)
                total = value if total is None else total + value
            return total

        up_ref[...] = panel(top, intersection).astype(jnp.bfloat16)
        fold_up.start()
        out_ref[...] = panel(low, inner)
        wide = STRIDE * GROUP_COLS
        not_low = jnp.where(me < count - 1, 1.0, 0.0)
        not_right = jnp.where(group < groups - 1, 1.0, 0.0)
        tail_rows = pl.ds(inner - intersection, intersection)

        def at_right(value):
            return jnp.concatenate([jnp.zeros((value.shape[0], side - intersection), jnp.float32), value[:, :intersection].astype(jnp.float32)], axis=1)

        fold_left.wait_recv()
        out_ref[:, wide - side:] = out_ref[:, wide - side:] + at_right(from_right_ref[...]) * not_right
        fold_up.wait_recv()
        out_ref[tail_rows, :] = out_ref[tail_rows, :] + from_down_ref[...].astype(jnp.float32) * not_low
        fold_corner.wait_recv()
        out_ref[tail_rows, wide - side:] = out_ref[tail_rows, wide - side:] + at_right(from_corner_ref[...]) * (not_right * not_low)

        for slot in range(slot_count):
            twin_copy(slot).wait_send()
            for piece in range(2):
                for who in range(2):
                    first_copy(slot, piece, who).wait_send()
        for piece in range(2):
            for hop in range(1, bits - 1):
                pack_copy(piece, hop).wait_send()
            sent(hand_ref.at[piece], final_ref.at[piece], final_sems, (piece,), across(1)).wait_send()
        fold_left.wait_send()
        fold_corner.wait_send()
        fold_up.wait_send()


def stitched_block(frames, masks, phases, own_tiles, otf, apod, intersection):
    slot_count, phase_count = (frames.shape[1], frames.shape[3])
    length = otf.shape[0]
    cells = masks.shape[-1]
    halfway = phase_count // 2
    right, left = tables(length, halfway)
    bands = halfway + 1
    count = lax.axis_size("ty")
    bits = count.bit_length() - 1
    part = length // 4
    wide = STRIDE * GROUP_COLS
    slot_rows = -(-slot_count // 8) * 8
    most = GROUP_COLS << (bits - 2)
    dma = pltpu.SemaphoreType.DMA

    def whole(array):
        return pl.BlockSpec(array.shape, lambda s: (0,) * array.ndim)

    return pl.pallas_call(
        lambda *refs: tile_kernel(phase_count, cells, intersection, slot_count, bits, *refs),
        grid=(slot_count,),
        in_specs=[
            pl.BlockSpec(memory_space=pltpu.SMEM),
            pl.BlockSpec(memory_space=pltpu.SMEM),
            pl.BlockSpec((1, 1) + frames.shape[2:], lambda s: (0, s, 0, 0, 0, 0)),
            pl.BlockSpec((1, 1, cells, cells), lambda s: (0, s, 0, 0)),
            whole(right), whole(left), whole(otf), whole(apod),
        ],
        out_specs=pl.BlockSpec((STRIDE, wide), lambda s: (0, 0)),
        out_shape=jax.ShapeDtypeStruct((STRIDE, wide), jnp.float32),
        scratch_shapes=[
            pltpu.VMEM((slot_rows, length), jnp.int32),
            pltpu.VMEM((2, length, length), jnp.float32),
            pltpu.VMEM((length, 2 * length), jnp.bfloat16),
            pltpu.VMEM((bands, 2 * length, 2 * length), jnp.bfloat16),
            pltpu.VMEM((2 * halfway + 1, length, length), jnp.float32),
            pltpu.VMEM((bands, length, 2 * length), jnp.bfloat16),
            pltpu.VMEM((bands, 2 * length, 2 * length), jnp.bfloat16),
            pltpu.VMEM((length, 2 * length), jnp.bfloat16),
            pltpu.VMEM((2 * length, length), jnp.bfloat16),
            pltpu.VMEM((slot_count, length, length), jnp.bfloat16),
            pltpu.VMEM((slot_count, 2 * part, length), jnp.bfloat16),
            pltpu.VMEM((2, slot_count, 2, part, length), jnp.bfloat16),
            pltpu.VMEM((5, slot_rows, length), jnp.int32),
            pltpu.VMEM((2, most, part, length), jnp.bfloat16),
            pltpu.VMEM((2, bits - 2, most, part, length), jnp.bfloat16),
            pltpu.VMEM((2, bits - 2, most, part, length), jnp.bfloat16),
            pltpu.VMEM((2, GROUP_COLS, part, length), jnp.bfloat16),
            pltpu.VMEM((2, GROUP_COLS, part, length), jnp.bfloat16),
            pltpu.VMEM((GROUP_COLS, length, length), jnp.bfloat16),
            pltpu.VMEM((intersection, wide), jnp.bfloat16),
            pltpu.VMEM((intersection, wide), jnp.bfloat16),
            pltpu.VMEM((length - intersection, 2 * intersection), jnp.bfloat16),
            pltpu.VMEM((intersection, 2 * intersection), jnp.bfloat16),
            dma((2, 5)),
            dma((2, slot_count)),
            dma((2, 2, slot_count, 2)),
            dma((2, 2, bits - 2)),
            dma((2, 2)),
            dma((2, 3)),
        ],
        compiler_params=pltpu.CompilerParams(
            vmem_limit_bytes=60 * 1024 * 1024, collective_id=0, has_side_effects=True
        ),
    )(phases.reshape(-1), own_tiles, frames, masks, right, left, otf, apod)


def shards(frames, masks, phases, slot_tile, otf, apod):
    length = otf.shape[0]
    intersection = length - STRIDE
    own_tiles = slot_tile[0]

    return stitched_block(frames, masks, phases, own_tiles, otf, apod, intersection)


def solution(mesh):
    in_specs = (
        P("tx", "ty", None, None, None, None),
        P("tx", "ty", None, None),
        P("tx", "ty", None),
        P("tx", "ty"),
        P(),
        P(),
    )
    out_specs = P("ty", "tx")
    return jax.shard_map(shards, mesh=mesh, in_specs=in_specs, out_specs=out_specs, check_vma=False)
```

```python
import math

import jax
import jax.numpy as jnp
import numpy as np
from jax import lax
from jax.experimental import pallas as pl
from jax.experimental.pallas import tpu as pltpu
from jax.sharding import PartitionSpec as P

STRIDE = 320
GROUP_COLS = 2


wiener = 0.1
pattern_base = (37, 101)
pattern_step = (29, -53)


def pattern_shift(orient):
    return (pattern_base[0] + orient * pattern_step[0], pattern_base[1] + orient * pattern_step[1])


def tables(length, halfway):
    places = np.arange(length)
    angles = (places[:, None] * places[None, :] % length) * (2.0 * math.pi / length)
    cosine, sine = (np.cos(angles), np.sin(angles))
    rows, cols = pattern_shift(0)
    right, left = [], []
    for m in range(halfway + 1):
        right.append(np.concatenate([np.roll(cosine, -m * cols, 1), -np.roll(sine, -m * cols, 1)], 1))
        left.append(np.concatenate([np.roll(cosine, -m * rows, 0), np.roll(sine, -m * rows, 0)], 1))
    return (
        jnp.asarray(np.stack(right).astype(jnp.bfloat16)),
        jnp.asarray(np.stack(left[1:]).astype(jnp.bfloat16)),
    )


def dot(a, b):
    return jnp.dot(a, b, preferred_element_type=jnp.float32)


def tile_kernel(
    phase_count, cells, intersection, slot_count, bits,
    phase_ref, tiles_ref, frames_ref, mask_ref, right_hbm, left_hbm, otf_ref, apod_ref,
    out_ref,
    table_sems, right_ref, left_ref, label_ref, flip_ref, left0_ref, wide_ref, gain_ref, images_ref, waves_ref, spec_ref, mid_ref, tile_ref, twin_ref, cand_ref,
    names_ref, keep_ref, pack_ref, land_ref, hand_ref, final_ref, full_ref, up_ref, from_down_ref,
    from_right_ref, from_corner_ref, name_sems, twin_sems, cand_sems, pack_sems, final_sems, fold_sems,
):
    me = lax.axis_index("ty")
    count = lax.axis_size("ty")
    group = lax.axis_index("tx")
    groups = lax.axis_size("tx")
    half = lax.rem(me, 2)
    routes = (tuple(range(1, bits)), tuple(reversed(range(1, bits))))

    def across(mask):
        other = me
        for bit in range(bits):
            if mask >> bit & 1:
                other = other + (1 << bit) - 2 * (1 << bit) * lax.rem(me // (1 << bit), 2)
        return (group, other)

    up = lax.rem(me + count - 1, count)
    down = lax.rem(me + 1, count)
    before = lax.rem(group + groups - 1, groups)
    after = lax.rem(group + 1, groups)
    name_masks = [1] + [(1 << route[0]) | low for route in routes for low in (0, 1)]
    greeted = [across(mask) for mask in name_masks]
    greeted += [across(1 << bit) for bit in range(2, bits - 1)]
    greeted += [(group, up), (group, down), (before, me), (after, me), (before, up), (after, down)]

    def sent(src, dst, sems, index, target):
        return pltpu.make_async_remote_copy(
            src_ref=src, dst_ref=dst, send_sem=sems.at[(0,) + index], recv_sem=sems.at[(1,) + index],
            device_id=target, device_id_type=pl.DeviceIdType.MESH,
        )

    step = pl.program_id(0)
    length = otf_ref.shape[-1]
    halfway = phase_count // 2
    shift_rows, shift_cols = pattern_shift(0)
    chunk = length // 3
    part = length // 4
    own_rows = pl.multiple_of(half * (2 * part), 2 * part)
    twin_rows = pl.multiple_of((1 - half) * (2 * part), 2 * part)

    def name_copy(place):
        return sent(label_ref, names_ref.at[place], name_sems, (place,), across(name_masks[place]))

    def twin_copy(slot):
        return sent(tile_ref.at[slot, pl.ds(twin_rows, 2 * part)], twin_ref.at[slot], twin_sems, (slot,), across(1))

    def first_copy(slot, piece, who):
        if who == 0:
            src = tile_ref.at[slot, pl.ds(pl.multiple_of(own_rows + piece * part, part), part)]
        else:
            src = twin_ref.at[slot, pl.ds(piece * part, part)]
        return sent(src, cand_ref.at[piece, slot, who], cand_sems, (piece, slot, who), across(1 << routes[piece][0]))

    def relay(slot):
        twin_copy(slot).wait_recv()
        for piece in range(2):
            first_copy(slot, piece, 1).start()

    @pl.when(step == 0)
    def _():
        barrier = pltpu.get_barrier_semaphore()
        for target in greeted:
            pl.semaphore_signal(barrier, inc=1, device_id=target, device_id_type=pl.DeviceIdType.MESH)
        pltpu.make_async_copy(right_hbm, right_ref, table_sems.at[0]).start()
        pltpu.make_async_copy(left_hbm, left_ref, table_sems.at[1]).start()

    @pl.when(step == 0)
    def _():
        index_sum = lax.broadcasted_iota(jnp.int32, (length, length), 0) + lax.broadcasted_iota(jnp.int32, (length, length), 1)
        swap = jnp.where((index_sum == 0) | (index_sum == length), 1.0, 0.0).astype(jnp.bfloat16)
        for place, source in enumerate((otf_ref, apod_ref)):
            value = source[...]
            high = value.astype(jnp.bfloat16)
            rest = (value - high.astype(jnp.float32)).astype(jnp.bfloat16)
            turned = None
            for piece in (high, rest):
                term = dot(dot(swap, piece).astype(jnp.bfloat16), swap)
                turned = term if turned is None else turned + term
            flip_ref[place] = turned

        for side in range(2):
            def rolled(m):
                value = otf_ref[...] if side == 0 else flip_ref[0]
                if m == 0:
                    return value
                value = pltpu.roll(value, (-m * shift_rows) % length, 0)
                return pltpu.roll(value, (-m * shift_cols) % length, 1)

            total = jnp.full((length, length), wiener, jnp.float32)
            for m in range(-halfway, halfway + 1):
                value = rolled(m)
                total = total + value * value
                if side == 0 and m >= 0:
                    gain_ref[m] = value
                if side == 1 and m > 0:
                    spec_side = value
                    mid_slot = halfway + m
                    gain_ref[mid_slot] = spec_side
            scale = (apod_ref[...] if side == 0 else flip_ref[1]) / total
            if side == 0:
                for m in range(halfway + 1):
                    gain_ref[m] = gain_ref[m] * scale
            else:
                for m in range(1, halfway + 1):
                    gain_ref[m] = gain_ref[m] + gain_ref[halfway + m] * scale

        pl.semaphore_wait(pltpu.get_barrier_semaphore(), len(greeted))
        label_ref[...] = jnp.full(label_ref.shape, -1, jnp.int32)
        for slot in range(slot_count):
            label_ref[slot:slot + 1, :] = jnp.full((1, length), tiles_ref[slot], jnp.int32)
        for place in range(len(name_masks)):
            name_copy(place).start()
        pltpu.make_async_copy(right_hbm, right_ref, table_sems.at[0]).wait()
        pltpu.make_async_copy(left_hbm, left_ref, table_sems.at[1]).wait()
        for m in range(1, halfway + 1):
            c, neg_s = (right_ref[m, :, :length], right_ref[m, :, length:])
            wide_ref[m, :length, :length] = c
            wide_ref[m, :length, length:] = neg_s
            wide_ref[m, length:, :length] = -neg_s
            wide_ref[m, length:, length:] = c
        c, neg_s = (right_ref[0, :, :length], right_ref[0, :, length:])
        wide_ref[0, :length, :length] = c
        wide_ref[0, :length, length:] = -neg_s
        wide_ref[0, length:, :length] = neg_s
        wide_ref[0, length:, length:] = c
        left0_ref[:, :length] = c
        left0_ref[:, length:] = -neg_s

    width = length // cells
    spread = jnp.where(
        lax.broadcasted_iota(jnp.int32, (cells, length), 1) // width
        == lax.broadcasted_iota(jnp.int32, (cells, length), 0), 1.0, 0.0).astype(jnp.bfloat16)
    mask_rows = dot(mask_ref[0, 0].astype(jnp.float32).astype(jnp.bfloat16), spread)
    places = (lax.broadcasted_iota(jnp.int32, (8, 128), 0), lax.broadcasted_iota(jnp.int32, (8, 128), 1))
    angles = places[0].astype(jnp.float32) * (
        phase_ref[step] + places[1].astype(jnp.float32) * (2.0 * math.pi / phase_count))
    coefs = (jnp.cos(angles) / phase_count, -jnp.sin(angles) / phase_count)
    weights = [[[jnp.broadcast_to(coefs[side][m:m + 1, p:p + 1], (width, length)) for p in range(phase_count)]
                for side in range(2)] for m in range(1, halfway + 1)]
    for cell in range(cells):
        rows = pl.ds(cell * width, width)
        keep = mask_rows[cell:cell + 1, :]
        planes = [frames_ref[0, 0, 0, p, rows, :].astype(jnp.float32) * keep for p in range(phase_count)]
        total = planes[0]
        for p in range(1, phase_count):
            total = total + planes[p]
        images_ref[0, rows, :length] = (total * (1.0 / phase_count)).astype(jnp.bfloat16)
        for m in range(1, halfway + 1):
            for side in range(2):
                weight = weights[m - 1][side]
                total = planes[0] * weight[0]
                for p in range(1, phase_count):
                    total = total + planes[p] * weight[p]
                images_ref[m, rows, side * length:(side + 1) * length] = total.astype(jnp.bfloat16)

    @pl.when(step > 0)
    def _():
        relay(step - 1)

    for m in range(halfway + 1):
        for third in range(3):
            rows = pl.ds(third * chunk, chunk)
            lower = pl.ds(length + third * chunk, chunk)
            if m == 0:
                wave = dot(images_ref[0, rows, :length], right_ref[0])
            else:
                wave = dot(images_ref[m, rows, :], wide_ref[m])
            wave = wave.astype(jnp.bfloat16)
            waves_ref[m, rows, :] = wave
            waves_ref[m, lower, :length] = wave[:, length:]
            waves_ref[m, lower, length:] = -wave[:, :length]

    for third in range(3):
        rows = pl.ds(third * chunk, chunk)
        total = None
        for m in range(halfway + 1):
            band = dot(left_ref[m - 1, rows, :] if m else left0_ref[rows, :], waves_ref[m])
            gain = gain_ref[m, rows, :]
            term = jnp.concatenate([gain, gain], axis=1) * band
            total = term if total is None else total + term
        spec_ref[rows, :] = total.astype(jnp.bfloat16)

    for third in range(3):
        rows = pl.ds(third * chunk, chunk)
        mid = dot(spec_ref[rows, :], wide_ref[0]).astype(jnp.bfloat16)
        mid_ref[rows, :] = mid[:, :length]
        mid_ref[pl.ds(length + third * chunk, chunk), :] = mid[:, length:]

    tile = tiles_ref[step]
    held = tile >= 0
    row_last = tile >= (count - 1) * GROUP_COLS
    column_last = lax.rem(jnp.maximum(tile, 0), GROUP_COLS) + GROUP_COLS * group == GROUP_COLS * groups - 1

    def ramp(places, is_last):
        places = places.astype(jnp.float32) + 0.5
        rising = jnp.minimum(places / intersection, 1.0)
        falling = jnp.minimum((length - places) / intersection, 1.0)
        return rising * jnp.where(is_last, jnp.ones_like(falling), falling)

    for third in range(3):
        rows = pl.ds(third * chunk, chunk)
        picture = dot(right_ref[0, rows, :], mid_ref[...]) * (1.0 / (length * length))
        places = lax.broadcasted_iota(jnp.int32, (chunk, length), 0) + third * chunk
        picture = picture * ramp(places, row_last)
        picture = picture * ramp(lax.broadcasted_iota(jnp.int32, (chunk, length), 1), column_last)
        tile_ref[step, rows, :] = jnp.where(held, picture, 0.0).astype(jnp.bfloat16)

    twin_copy(step).start()
    for piece in range(2):
        first_copy(step, piece, 0).start()

    @pl.when(step == slot_count - 1)
    def _():
        relay(slot_count - 1)
        for place in range(len(name_masks)):
            name_copy(place).wait()

        def candidate(piece, who, slot):
            if who == 0:
                return tile_ref[slot, pl.ds(pl.multiple_of(own_rows + piece * part, part), part), :]
            if who == 1:
                return twin_ref[slot, pl.ds(piece * part, part), :]
            return cand_ref[piece, slot, who - 2]

        def labels(piece, who, slot):
            if who == 0:
                return label_ref[slot:slot + 1, :]
            place = 0 if who == 1 else 1 + 2 * piece + (who - 2)
            return names_ref[place, slot:slot + 1, :]

        def combos(free):
            masks = [0]
            for bit in free:
                masks = masks + [mask | (1 << bit) for mask in masks]
            return masks

        def packed(piece, mask, column, sources):
            wanted = across(mask)[1] * GROUP_COLS + column
            total = None
            for slot, who in sources:
                hit = jnp.where(labels(piece, who, slot) == wanted, 1.0, 0.0).astype(jnp.bfloat16)
                term = candidate(piece, who, slot) * hit
                total = term if total is None else total + term
            return total

        def pack_copy(piece, hop, low):
            size = GROUP_COLS << (len(routes[piece]) - hop - 1)
            there = pl.ds(low * size, size)
            return sent(
                pack_ref.at[piece, hop - 1, there], land_ref.at[piece, hop - 1, there],
                pack_sems, (piece, hop - 1, low), across(1 << routes[piece][hop]),
            )

        def final_copy(piece):
            return sent(hand_ref.at[piece], final_ref.at[piece], final_sems, (piece,), across(1))

        last = slot_count - 1
        early = [(slot, who) for slot in range(last) for who in range(4)] + [(last, 0), (last, 1)]
        late = [(last, 2), (last, 3)]
        rests = [combos(route[2:] + (0,)) for route in routes]
        for piece in range(2):
            for slot in range(last):
                for who in range(2):
                    first_copy(slot, piece, who).wait_recv()
        for piece in range(2):
            for place, mask in enumerate(rests[piece]):
                for column in range(GROUP_COLS):
                    index = place * GROUP_COLS + column
                    pack_ref[piece, 0, index] = packed(piece, mask | (1 << routes[piece][1]), column, early)
        for piece in range(2):
            for who in range(2):
                first_copy(last, piece, who).wait_recv()
        for low in (1, 0):
            for piece in range(2):
                for place, mask in enumerate(rests[piece]):
                    if mask & 1 == low:
                        for column in range(GROUP_COLS):
                            index = place * GROUP_COLS + column
                            pack_ref[piece, 0, index] = pack_ref[piece, 0, index] + packed(
                                piece, mask | (1 << routes[piece][1]), column, late)
                pack_copy(piece, 1, low).start()
        for low in (1, 0):
            for piece in range(2):
                for place, mask in enumerate(rests[piece]):
                    if mask & 1 == low:
                        for column in range(GROUP_COLS):
                            keep_ref[piece, place * GROUP_COLS + column] = packed(piece, mask, column, early + late)
        for hop in range(1, bits - 2):
            for piece in range(2):
                for low in (1, 0):
                    pack_copy(piece, hop, low).wait_recv()
                held_order = combos(routes[piece][hop + 1:] + (0,))
                bit = 1 << routes[piece][hop + 1]
                for place, mask in enumerate(combos(routes[piece][hop + 2:] + (0,))):
                    there = held_order.index(mask | bit)
                    here = held_order.index(mask)
                    for column in range(GROUP_COLS):
                        i, j, k = (there * GROUP_COLS + column, here * GROUP_COLS + column, place * GROUP_COLS + column)
                        pack_ref[piece, hop, k] = keep_ref[piece, i] + land_ref[piece, hop - 1, i]
                        keep_ref[piece, k] = keep_ref[piece, j] + land_ref[piece, hop - 1, j]
                for low in (1, 0):
                    pack_copy(piece, hop + 1, low).start()
        for piece in range(2):
            pack_copy(piece, bits - 2, 1).wait_recv()
            for column in range(GROUP_COLS):
                hand_ref[piece, column] = keep_ref[piece, GROUP_COLS + column] + land_ref[piece, bits - 3, GROUP_COLS + column]
            final_copy(piece).start()
        for piece in range(2):
            pack_copy(piece, bits - 2, 0).wait_recv()
            rows = pl.ds(pl.multiple_of(own_rows + piece * part, part), part)
            for column in range(GROUP_COLS):
                full_ref[column, rows, :] = keep_ref[piece, column] + land_ref[piece, bits - 3, column]
        for piece in range(2):
            final_copy(piece).wait_recv()
            rows = pl.ds(pl.multiple_of(twin_rows + piece * part, part), part)
            for column in range(GROUP_COLS):
                full_ref[column, rows, :] = final_ref[piece, column]

        side = 2 * intersection
        inner = length - intersection
        top = pl.ds(0, intersection)
        low = pl.ds(intersection, inner)

        fold_left = sent(full_ref.at[0, low, pl.ds(0, side)], from_right_ref, fold_sems, (0,), (before, me))
        fold_corner = sent(full_ref.at[0, top, pl.ds(0, side)], from_corner_ref, fold_sems, (1,), (before, up))
        fold_up = sent(up_ref, from_down_ref, fold_sems, (2,), (group, up))
        fold_left.start()
        fold_corner.start()

        def panel(rows, size):
            total = None
            for column in range(GROUP_COLS):
                value = full_ref[column, rows, :].astype(jnp.float32)
                start = STRIDE * column - intersection
                if start < 0:
                    value = value[:, -start:]
                    start = 0
                ends = [jnp.zeros((size, start), jnp.float32), value]
                ends.append(jnp.zeros((size, STRIDE * GROUP_COLS - start - value.shape[1]), jnp.float32))
                value = jnp.concatenate([piece for piece in ends if piece.shape[1]], axis=1)
                total = value if total is None else total + value
            return total

        up_ref[...] = panel(top, intersection).astype(jnp.bfloat16)
        fold_up.start()
        out_ref[...] = panel(low, inner)
        wide = STRIDE * GROUP_COLS
        not_low = jnp.where(me < count - 1, 1.0, 0.0)
        not_right = jnp.where(group < groups - 1, 1.0, 0.0)
        tail_rows = pl.ds(inner - intersection, intersection)

        def at_right(value):
            return jnp.concatenate([jnp.zeros((value.shape[0], side - intersection), jnp.float32), value[:, :intersection].astype(jnp.float32)], axis=1)

        fold_left.wait_recv()
        out_ref[:, wide - side:] = out_ref[:, wide - side:] + at_right(from_right_ref[...]) * not_right
        fold_up.wait_recv()
        out_ref[tail_rows, :] = out_ref[tail_rows, :] + from_down_ref[...].astype(jnp.float32) * not_low
        fold_corner.wait_recv()
        out_ref[tail_rows, wide - side:] = out_ref[tail_rows, wide - side:] + at_right(from_corner_ref[...]) * (not_right * not_low)

        for slot in range(slot_count):
            twin_copy(slot).wait_send()
            for piece in range(2):
                for who in range(2):
                    first_copy(slot, piece, who).wait_send()
        for piece in range(2):
            for hop in range(1, bits - 1):
                for low in range(2):
                    pack_copy(piece, hop, low).wait_send()
            final_copy(piece).wait_send()
        fold_left.wait_send()
        fold_corner.wait_send()
        fold_up.wait_send()


def stitched_block(frames, masks, phases, own_tiles, otf, apod, intersection):
    slot_count, phase_count = (frames.shape[1], frames.shape[3])
    length = otf.shape[0]
    cells = masks.shape[-1]
    halfway = phase_count // 2
    right, left = tables(length, halfway)
    bands = halfway + 1
    count = lax.axis_size("ty")
    bits = count.bit_length() - 1
    part = length // 4
    wide = STRIDE * GROUP_COLS
    slot_rows = -(-slot_count // 8) * 8
    most = GROUP_COLS << (bits - 2)
    dma = pltpu.SemaphoreType.DMA

    def whole(array):
        return pl.BlockSpec(array.shape, lambda s: (0,) * array.ndim)

    return pl.pallas_call(
        lambda *refs: tile_kernel(phase_count, cells, intersection, slot_count, bits, *refs),
        grid=(slot_count,),
        in_specs=[
            pl.BlockSpec(memory_space=pltpu.SMEM),
            pl.BlockSpec(memory_space=pltpu.SMEM),
            pl.BlockSpec((1, 1) + frames.shape[2:], lambda s: (0, s, 0, 0, 0, 0)),
            pl.BlockSpec((1, 1, cells, cells), lambda s: (0, s, 0, 0)),
            pl.BlockSpec(memory_space=pl.ANY), pl.BlockSpec(memory_space=pl.ANY), whole(otf), whole(apod),
        ],
        out_specs=pl.BlockSpec((STRIDE, wide), lambda s: (0, 0)),
        out_shape=jax.ShapeDtypeStruct((STRIDE, wide), jnp.float32),
        scratch_shapes=[
            dma((2,)),
            pltpu.VMEM(right.shape, jnp.bfloat16),
            pltpu.VMEM(left.shape, jnp.bfloat16),
            pltpu.VMEM((slot_rows, length), jnp.int32),
            pltpu.VMEM((2, length, length), jnp.float32),
            pltpu.VMEM((length, 2 * length), jnp.bfloat16),
            pltpu.VMEM((bands, 2 * length, 2 * length), jnp.bfloat16),
            pltpu.VMEM((2 * halfway + 1, length, length), jnp.float32),
            pltpu.VMEM((bands, length, 2 * length), jnp.bfloat16),
            pltpu.VMEM((bands, 2 * length, 2 * length), jnp.bfloat16),
            pltpu.VMEM((length, 2 * length), jnp.bfloat16),
            pltpu.VMEM((2 * length, length), jnp.bfloat16),
            pltpu.VMEM((slot_count, length, length), jnp.bfloat16),
            pltpu.VMEM((slot_count, 2 * part, length), jnp.bfloat16),
            pltpu.VMEM((2, slot_count, 2, part, length), jnp.bfloat16),
            pltpu.VMEM((5, slot_rows, length), jnp.int32),
            pltpu.VMEM((2, most, part, length), jnp.bfloat16),
            pltpu.VMEM((2, bits - 2, most, part, length), jnp.bfloat16),
            pltpu.VMEM((2, bits - 2, most, part, length), jnp.bfloat16),
            pltpu.VMEM((2, GROUP_COLS, part, length), jnp.bfloat16),
            pltpu.VMEM((2, GROUP_COLS, part, length), jnp.bfloat16),
            pltpu.VMEM((GROUP_COLS, length, length), jnp.bfloat16),
            pltpu.VMEM((intersection, wide), jnp.bfloat16),
            pltpu.VMEM((intersection, wide), jnp.bfloat16),
            pltpu.VMEM((length - intersection, 2 * intersection), jnp.bfloat16),
            pltpu.VMEM((intersection, 2 * intersection), jnp.bfloat16),
            dma((2, 5)),
            dma((2, slot_count)),
            dma((2, 2, slot_count, 2)),
            dma((2, 2, bits - 2, 2)),
            dma((2, 2)),
            dma((2, 3)),
        ],
        compiler_params=pltpu.CompilerParams(
            vmem_limit_bytes=60 * 1024 * 1024, collective_id=0, has_side_effects=True
        ),
    )(phases.reshape(-1), own_tiles, frames, masks, right, left, otf, apod)


def shards(frames, masks, phases, slot_tile, otf, apod):
    length = otf.shape[0]
    intersection = length - STRIDE
    own_tiles = slot_tile[0]

    return stitched_block(frames, masks, phases, own_tiles, otf, apod, intersection)


def solution(mesh):
    in_specs = (
        P("tx", "ty", None, None, None, None),
        P("tx", "ty", None, None),
        P("tx", "ty", None),
        P("tx", "ty"),
        P(),
        P(),
    )
    out_specs = P("ty", "tx")
    return jax.shard_map(shards, mesh=mesh, in_specs=in_specs, out_specs=out_specs, check_vma=False)
```

```python
import math

import jax
import jax.numpy as jnp
import numpy as np
from jax import lax
from jax.experimental import pallas as pl
from jax.experimental.pallas import tpu as pltpu
from jax.sharding import PartitionSpec as P

STRIDE = 320
GROUP_COLS = 2


wiener = 0.1
pattern_base = (37, 101)
pattern_step = (29, -53)


def pattern_shift(orient):
    return (pattern_base[0] + orient * pattern_step[0], pattern_base[1] + orient * pattern_step[1])


def tables(length, halfway):
    places = np.arange(length)
    angles = (places[:, None] * places[None, :] % length) * (2.0 * math.pi / length)
    cosine, sine = (np.cos(angles), np.sin(angles))
    rows, cols = pattern_shift(0)
    right, left = [], []
    for m in range(halfway + 1):
        right.append(np.concatenate([np.roll(cosine, -m * cols, 1), -np.roll(sine, -m * cols, 1)], 1))
        left.append(np.concatenate([np.roll(cosine, -m * rows, 0), np.roll(sine, -m * rows, 0)], 1))
    return (
        jnp.asarray(np.stack(right).astype(jnp.bfloat16)),
        jnp.asarray(np.stack(left[1:]).astype(jnp.bfloat16)),
    )


def dot(a, b):
    return jnp.dot(a, b, preferred_element_type=jnp.float32)


def tile_kernel(
    phase_count, cells, intersection, slot_count, bits,
    phase_ref, tiles_ref, frames_ref, mask_ref, right_hbm, left_hbm, otf_ref, apod_ref,
    out_ref,
    table_sems, right_ref, left_ref, label_ref, flip_ref, left0_ref, wide_ref, gain_ref, images_ref, waves_ref, spec_ref, mid_ref, tile_ref, twin_ref, cand_ref,
    names_ref, keep_ref, pack_ref, land_ref, hand_ref, final_ref, full_ref, up_ref, from_down_ref,
    from_right_ref, from_corner_ref, name_sems, twin_sems, cand_sems, pack_sems, final_sems, fold_sems,
):
    me = lax.axis_index("ty")
    count = lax.axis_size("ty")
    group = lax.axis_index("tx")
    groups = lax.axis_size("tx")
    half = lax.rem(me, 2)
    routes = (tuple(range(1, bits)), tuple(reversed(range(1, bits))))

    def across(mask):
        other = me
        for bit in range(bits):
            if mask >> bit & 1:
                other = other + (1 << bit) - 2 * (1 << bit) * lax.rem(me // (1 << bit), 2)
        return (group, other)

    up = lax.rem(me + count - 1, count)
    down = lax.rem(me + 1, count)
    before = lax.rem(group + groups - 1, groups)
    after = lax.rem(group + 1, groups)
    name_masks = [1] + [(1 << route[0]) | low for route in routes for low in (0, 1)]
    greeted = [across(mask) for mask in name_masks]
    greeted += [across(1 << bit) for bit in range(2, bits - 1)]
    greeted += [(group, up), (group, down), (before, me), (after, me), (before, up), (after, down)]

    def sent(src, dst, sems, index, target):
        return pltpu.make_async_remote_copy(
            src_ref=src, dst_ref=dst, send_sem=sems.at[(0,) + index], recv_sem=sems.at[(1,) + index],
            device_id=target, device_id_type=pl.DeviceIdType.MESH,
        )

    step = pl.program_id(0)
    length = otf_ref.shape[-1]
    halfway = phase_count // 2
    shift_rows, shift_cols = pattern_shift(0)
    chunk = length // 3
    part = length // 4
    own_rows = pl.multiple_of(half * (2 * part), 2 * part)
    twin_rows = pl.multiple_of((1 - half) * (2 * part), 2 * part)

    def name_copy(place):
        return sent(label_ref, names_ref.at[place], name_sems, (place,), across(name_masks[place]))

    def twin_copy(slot):
        return sent(tile_ref.at[slot, pl.ds(twin_rows, 2 * part)], twin_ref.at[slot], twin_sems, (slot,), across(1))

    def first_copy(slot, piece, who):
        if who == 0:
            src = tile_ref.at[slot, pl.ds(pl.multiple_of(own_rows + piece * part, part), part)]
        else:
            src = twin_ref.at[slot, pl.ds(piece * part, part)]
        return sent(src, cand_ref.at[piece, slot, who], cand_sems, (piece, slot, who), across(1 << routes[piece][0]))

    def relay(slot):
        twin_copy(slot).wait_recv()
        for piece in range(2):
            first_copy(slot, piece, 1).start()

    @pl.when(step == 0)
    def _():
        barrier = pltpu.get_barrier_semaphore()
        for target in greeted:
            pl.semaphore_signal(barrier, inc=1, device_id=target, device_id_type=pl.DeviceIdType.MESH)
        pltpu.make_async_copy(right_hbm, right_ref, table_sems.at[0]).start()
        pltpu.make_async_copy(left_hbm, left_ref, table_sems.at[1]).start()

    @pl.when(step == 0)
    def _():
        index_sum = lax.broadcasted_iota(jnp.int32, (length, length), 0) + lax.broadcasted_iota(jnp.int32, (length, length), 1)
        swap = jnp.where((index_sum == 0) | (index_sum == length), 1.0, 0.0).astype(jnp.bfloat16)
        for place, source in enumerate((otf_ref, apod_ref)):
            value = source[...]
            high = value.astype(jnp.bfloat16)
            rest = (value - high.astype(jnp.float32)).astype(jnp.bfloat16)
            turned = None
            for piece in (high, rest):
                term = dot(dot(swap, piece).astype(jnp.bfloat16), swap)
                turned = term if turned is None else turned + term
            flip_ref[place] = turned

        for side in range(2):
            def rolled(m):
                value = otf_ref[...] if side == 0 else flip_ref[0]
                if m == 0:
                    return value
                value = pltpu.roll(value, (-m * shift_rows) % length, 0)
                return pltpu.roll(value, (-m * shift_cols) % length, 1)

            total = jnp.full((length, length), wiener, jnp.float32)
            for m in range(-halfway, halfway + 1):
                value = rolled(m)
                total = total + value * value
                if side == 0 and m >= 0:
                    gain_ref[m] = value
                if side == 1 and m > 0:
                    spec_side = value
                    mid_slot = halfway + m
                    gain_ref[mid_slot] = spec_side
            scale = (apod_ref[...] if side == 0 else flip_ref[1]) / total
            if side == 0:
                for m in range(halfway + 1):
                    gain_ref[m] = gain_ref[m] * scale
            else:
                for m in range(1, halfway + 1):
                    gain_ref[m] = gain_ref[m] + gain_ref[halfway + m] * scale

        pl.semaphore_wait(pltpu.get_barrier_semaphore(), len(greeted))
        label_ref[...] = jnp.full(label_ref.shape, -1, jnp.int32)
        for slot in range(slot_count):
            label_ref[slot:slot + 1, :] = jnp.full((1, length), tiles_ref[slot], jnp.int32)
        for place in range(len(name_masks)):
            name_copy(place).start()
        pltpu.make_async_copy(right_hbm, right_ref, table_sems.at[0]).wait()
        pltpu.make_async_copy(left_hbm, left_ref, table_sems.at[1]).wait()
        for m in range(1, halfway + 1):
            c, neg_s = (right_ref[m, :, :length], right_ref[m, :, length:])
            wide_ref[m, :length, :length] = c
            wide_ref[m, :length, length:] = neg_s
            wide_ref[m, length:, :length] = -neg_s
            wide_ref[m, length:, length:] = c
        c, neg_s = (right_ref[0, :, :length], right_ref[0, :, length:])
        wide_ref[0, :length, :length] = c
        wide_ref[0, :length, length:] = -neg_s
        wide_ref[0, length:, :length] = neg_s
        wide_ref[0, length:, length:] = c
        left0_ref[:, :length] = c
        left0_ref[:, length:] = -neg_s

    width = length // cells
    spread = jnp.where(
        lax.broadcasted_iota(jnp.int32, (cells, length), 1) // width
        == lax.broadcasted_iota(jnp.int32, (cells, length), 0), 1.0, 0.0).astype(jnp.bfloat16)
    mask_rows = dot(mask_ref[0, :, 0, :].astype(jnp.float32).astype(jnp.bfloat16), spread)
    places = (lax.broadcasted_iota(jnp.int32, (8, 128), 0), lax.broadcasted_iota(jnp.int32, (8, 128), 1))
    angles = places[0].astype(jnp.float32) * (
        phase_ref[step] + places[1].astype(jnp.float32) * (2.0 * math.pi / phase_count))
    coefs = (jnp.cos(angles) / phase_count, -jnp.sin(angles) / phase_count)
    weights = [[[jnp.broadcast_to(coefs[side][m:m + 1, p:p + 1], (width, length)) for p in range(phase_count)]
                for side in range(2)] for m in range(1, halfway + 1)]
    def mix(cell):
        rows = pl.ds(cell * width, width)
        keep = mask_rows[cell:cell + 1, :]
        planes = [frames_ref[0, 0, 0, p, rows, :].astype(jnp.float32) * keep for p in range(phase_count)]
        total = planes[0]
        for p in range(1, phase_count):
            total = total + planes[p]
        images_ref[0, rows, :length] = (total * (1.0 / phase_count)).astype(jnp.bfloat16)
        for m in range(1, halfway + 1):
            for side in range(2):
                weight = weights[m - 1][side]
                total = planes[0] * weight[0]
                for p in range(1, phase_count):
                    total = total + planes[p] * weight[p]
                images_ref[m, rows, side * length:(side + 1) * length] = total.astype(jnp.bfloat16)

    for third in range(3):
        rows = pl.ds(third * chunk, chunk)
        lower = pl.ds(length + third * chunk, chunk)
        for cell in range(third * cells // 3, (third + 1) * cells // 3):
            mix(cell)
        for m in range(halfway + 1):
            if m == 0:
                wave = dot(images_ref[0, rows, :length], right_ref[0])
            else:
                wave = dot(images_ref[m, rows, :], wide_ref[m])
            wave = wave.astype(jnp.bfloat16)
            waves_ref[m, rows, :] = wave
            waves_ref[m, lower, :length] = wave[:, length:]
            waves_ref[m, lower, length:] = -wave[:, :length]

    @pl.when(step > 0)
    def _():
        relay(step - 1)

    for third in range(3):
        rows = pl.ds(third * chunk, chunk)
        total = None
        for m in range(halfway + 1):
            band = dot(left_ref[m - 1, rows, :] if m else left0_ref[rows, :], waves_ref[m])
            gain = gain_ref[m, rows, :]
            term = jnp.concatenate([gain, gain], axis=1) * band
            total = term if total is None else total + term
        spec_ref[rows, :] = total.astype(jnp.bfloat16)

    for third in range(3):
        rows = pl.ds(third * chunk, chunk)
        mid = dot(spec_ref[rows, :], wide_ref[0]).astype(jnp.bfloat16)
        mid_ref[rows, :] = mid[:, :length]
        mid_ref[pl.ds(length + third * chunk, chunk), :] = mid[:, length:]

    tile = tiles_ref[step]
    held = tile >= 0
    row_last = tile >= (count - 1) * GROUP_COLS
    column_last = lax.rem(jnp.maximum(tile, 0), GROUP_COLS) + GROUP_COLS * group == GROUP_COLS * groups - 1

    def ramp(places, is_last):
        places = places.astype(jnp.float32) + 0.5
        rising = jnp.minimum(places / intersection, 1.0)
        falling = jnp.minimum((length - places) / intersection, 1.0)
        return rising * jnp.where(is_last, jnp.ones_like(falling), falling)

    for third in range(3):
        rows = pl.ds(third * chunk, chunk)
        picture = dot(right_ref[0, rows, :], mid_ref[...]) * (1.0 / (length * length))
        places = lax.broadcasted_iota(jnp.int32, (chunk, length), 0) + third * chunk
        picture = picture * ramp(places, row_last)
        picture = picture * ramp(lax.broadcasted_iota(jnp.int32, (chunk, length), 1), column_last)
        tile_ref[step, rows, :] = jnp.where(held, picture, 0.0).astype(jnp.bfloat16)

    twin_copy(step).start()
    for piece in range(2):
        first_copy(step, piece, 0).start()

    @pl.when(step == slot_count - 1)
    def _():
        relay(slot_count - 1)
        for place in range(len(name_masks)):
            name_copy(place).wait()

        def candidate(piece, who, slot):
            if who == 0:
                return tile_ref[slot, pl.ds(pl.multiple_of(own_rows + piece * part, part), part), :]
            if who == 1:
                return twin_ref[slot, pl.ds(piece * part, part), :]
            return cand_ref[piece, slot, who - 2]

        def labels(piece, who, slot):
            if who == 0:
                return label_ref[slot:slot + 1, :]
            place = 0 if who == 1 else 1 + 2 * piece + (who - 2)
            return names_ref[place, slot:slot + 1, :]

        def combos(free):
            masks = [0]
            for bit in free:
                masks = masks + [mask | (1 << bit) for mask in masks]
            return masks

        def packed(piece, mask, column, sources):
            wanted = across(mask)[1] * GROUP_COLS + column
            total = None
            for slot, who in sources:
                hit = jnp.where(labels(piece, who, slot) == wanted, 1.0, 0.0).astype(jnp.bfloat16)
                term = candidate(piece, who, slot) * hit
                total = term if total is None else total + term
            return total

        def pack_copy(piece, hop, low):
            size = GROUP_COLS << (len(routes[piece]) - hop - 1)
            there = pl.ds(low * size, size)
            return sent(
                pack_ref.at[piece, hop - 1, there], land_ref.at[piece, hop - 1, there],
                pack_sems, (piece, hop - 1, low), across(1 << routes[piece][hop]),
            )

        def final_copy(piece):
            return sent(hand_ref.at[piece], final_ref.at[piece], final_sems, (piece,), across(1))

        last = slot_count - 1
        early = [(slot, who) for slot in range(last) for who in range(4)] + [(last, 0), (last, 1)]
        late = [(last, 2), (last, 3)]
        rests = [combos(route[2:] + (0,)) for route in routes]
        for piece in range(2):
            for slot in range(last):
                for who in range(2):
                    first_copy(slot, piece, who).wait_recv()
        for piece in range(2):
            for place, mask in enumerate(rests[piece]):
                for column in range(GROUP_COLS):
                    index = place * GROUP_COLS + column
                    pack_ref[piece, 0, index] = packed(piece, mask | (1 << routes[piece][1]), column, early)
        for piece in range(2):
            for who in range(2):
                first_copy(last, piece, who).wait_recv()
        for low in (1, 0):
            for piece in range(2):
                for place, mask in enumerate(rests[piece]):
                    if mask & 1 == low:
                        for column in range(GROUP_COLS):
                            index = place * GROUP_COLS + column
                            pack_ref[piece, 0, index] = pack_ref[piece, 0, index] + packed(
                                piece, mask | (1 << routes[piece][1]), column, late)
                pack_copy(piece, 1, low).start()
        for low in (1, 0):
            for piece in range(2):
                for place, mask in enumerate(rests[piece]):
                    if mask & 1 == low:
                        for column in range(GROUP_COLS):
                            keep_ref[piece, place * GROUP_COLS + column] = packed(piece, mask, column, early + late)
        for hop in range(1, bits - 2):
            for piece in range(2):
                for low in (1, 0):
                    pack_copy(piece, hop, low).wait_recv()
                held_order = combos(routes[piece][hop + 1:] + (0,))
                bit = 1 << routes[piece][hop + 1]
                for place, mask in enumerate(combos(routes[piece][hop + 2:] + (0,))):
                    there = held_order.index(mask | bit)
                    here = held_order.index(mask)
                    for column in range(GROUP_COLS):
                        i, j, k = (there * GROUP_COLS + column, here * GROUP_COLS + column, place * GROUP_COLS + column)
                        pack_ref[piece, hop, k] = keep_ref[piece, i] + land_ref[piece, hop - 1, i]
                        keep_ref[piece, k] = keep_ref[piece, j] + land_ref[piece, hop - 1, j]
                for low in (1, 0):
                    pack_copy(piece, hop + 1, low).start()
        for piece in range(2):
            pack_copy(piece, bits - 2, 1).wait_recv()
            for column in range(GROUP_COLS):
                hand_ref[piece, column] = keep_ref[piece, GROUP_COLS + column] + land_ref[piece, bits - 3, GROUP_COLS + column]
            final_copy(piece).start()
        for piece in range(2):
            pack_copy(piece, bits - 2, 0).wait_recv()
            rows = pl.ds(pl.multiple_of(own_rows + piece * part, part), part)
            for column in range(GROUP_COLS):
                full_ref[column, rows, :] = keep_ref[piece, column] + land_ref[piece, bits - 3, column]
        for piece in range(2):
            final_copy(piece).wait_recv()
            rows = pl.ds(pl.multiple_of(twin_rows + piece * part, part), part)
            for column in range(GROUP_COLS):
                full_ref[column, rows, :] = final_ref[piece, column]

        side = 2 * intersection
        inner = length - intersection
        top = pl.ds(0, intersection)
        low = pl.ds(intersection, inner)

        fold_left = sent(full_ref.at[0, low, pl.ds(0, side)], from_right_ref, fold_sems, (0,), (before, me))
        fold_corner = sent(full_ref.at[0, top, pl.ds(0, side)], from_corner_ref, fold_sems, (1,), (before, up))
        fold_up = sent(up_ref, from_down_ref, fold_sems, (2,), (group, up))
        fold_left.start()
        fold_corner.start()

        def panel(rows, size):
            total = None
            for column in range(GROUP_COLS):
                value = full_ref[column, rows, :].astype(jnp.float32)
                start = STRIDE * column - intersection
                if start < 0:
                    value = value[:, -start:]
                    start = 0
                ends = [jnp.zeros((size, start), jnp.float32), value]
                ends.append(jnp.zeros((size, STRIDE * GROUP_COLS - start - value.shape[1]), jnp.float32))
                value = jnp.concatenate([piece for piece in ends if piece.shape[1]], axis=1)
                total = value if total is None else total + value
            return total

        up_ref[...] = panel(top, intersection).astype(jnp.bfloat16)
        fold_up.start()
        out_ref[...] = panel(low, inner)
        wide = STRIDE * GROUP_COLS
        not_low = jnp.where(me < count - 1, 1.0, 0.0)
        not_right = jnp.where(group < groups - 1, 1.0, 0.0)
        tail_rows = pl.ds(inner - intersection, intersection)

        def at_right(value):
            return jnp.concatenate([jnp.zeros((value.shape[0], side - intersection), jnp.float32), value[:, :intersection].astype(jnp.float32)], axis=1)

        fold_left.wait_recv()
        out_ref[:, wide - side:] = out_ref[:, wide - side:] + at_right(from_right_ref[...]) * not_right
        fold_up.wait_recv()
        out_ref[tail_rows, :] = out_ref[tail_rows, :] + from_down_ref[...].astype(jnp.float32) * not_low
        fold_corner.wait_recv()
        out_ref[tail_rows, wide - side:] = out_ref[tail_rows, wide - side:] + at_right(from_corner_ref[...]) * (not_right * not_low)

        for slot in range(slot_count):
            twin_copy(slot).wait_send()
            for piece in range(2):
                for who in range(2):
                    first_copy(slot, piece, who).wait_send()
        for piece in range(2):
            for hop in range(1, bits - 1):
                for low in range(2):
                    pack_copy(piece, hop, low).wait_send()
            final_copy(piece).wait_send()
        fold_left.wait_send()
        fold_corner.wait_send()
        fold_up.wait_send()


def stitched_block(frames, masks, phases, own_tiles, otf, apod, intersection):
    slot_count, phase_count = (frames.shape[1], frames.shape[3])
    length = otf.shape[0]
    cells = masks.shape[-1]
    halfway = phase_count // 2
    right, left = tables(length, halfway)
    bands = halfway + 1
    count = lax.axis_size("ty")
    bits = count.bit_length() - 1
    part = length // 4
    wide = STRIDE * GROUP_COLS
    slot_rows = -(-slot_count // 8) * 8
    most = GROUP_COLS << (bits - 2)
    dma = pltpu.SemaphoreType.DMA

    def whole(array):
        return pl.BlockSpec(array.shape, lambda s: (0,) * array.ndim)

    return pl.pallas_call(
        lambda *refs: tile_kernel(phase_count, cells, intersection, slot_count, bits, *refs),
        grid=(slot_count,),
        in_specs=[
            pl.BlockSpec(memory_space=pltpu.SMEM),
            pl.BlockSpec(memory_space=pltpu.SMEM),
            pl.BlockSpec((1, 1) + frames.shape[2:], lambda s: (0, s, 0, 0, 0, 0)),
            pl.BlockSpec((1, cells, 1, cells), lambda s: (s, 0, 0, 0)),
            pl.BlockSpec(memory_space=pl.ANY), pl.BlockSpec(memory_space=pl.ANY), whole(otf), whole(apod),
        ],
        out_specs=pl.BlockSpec((STRIDE, wide), lambda s: (0, 0)),
        out_shape=jax.ShapeDtypeStruct((STRIDE, wide), jnp.float32),
        scratch_shapes=[
            dma((2,)),
            pltpu.VMEM(right.shape, jnp.bfloat16),
            pltpu.VMEM(left.shape, jnp.bfloat16),
            pltpu.VMEM((slot_rows, length), jnp.int32),
            pltpu.VMEM((2, length, length), jnp.float32),
            pltpu.VMEM((length, 2 * length), jnp.bfloat16),
            pltpu.VMEM((bands, 2 * length, 2 * length), jnp.bfloat16),
            pltpu.VMEM((2 * halfway + 1, length, length), jnp.float32),
            pltpu.VMEM((bands, length, 2 * length), jnp.bfloat16),
            pltpu.VMEM((bands, 2 * length, 2 * length), jnp.bfloat16),
            pltpu.VMEM((length, 2 * length), jnp.bfloat16),
            pltpu.VMEM((2 * length, length), jnp.bfloat16),
            pltpu.VMEM((slot_count, length, length), jnp.bfloat16),
            pltpu.VMEM((slot_count, 2 * part, length), jnp.bfloat16),
            pltpu.VMEM((2, slot_count, 2, part, length), jnp.bfloat16),
            pltpu.VMEM((5, slot_rows, length), jnp.int32),
            pltpu.VMEM((2, most, part, length), jnp.bfloat16),
            pltpu.VMEM((2, bits - 2, most, part, length), jnp.bfloat16),
            pltpu.VMEM((2, bits - 2, most, part, length), jnp.bfloat16),
            pltpu.VMEM((2, GROUP_COLS, part, length), jnp.bfloat16),
            pltpu.VMEM((2, GROUP_COLS, part, length), jnp.bfloat16),
            pltpu.VMEM((GROUP_COLS, length, length), jnp.bfloat16),
            pltpu.VMEM((intersection, wide), jnp.bfloat16),
            pltpu.VMEM((intersection, wide), jnp.bfloat16),
            pltpu.VMEM((length - intersection, 2 * intersection), jnp.bfloat16),
            pltpu.VMEM((intersection, 2 * intersection), jnp.bfloat16),
            dma((2, 5)),
            dma((2, slot_count)),
            dma((2, 2, slot_count, 2)),
            dma((2, 2, bits - 2, 2)),
            dma((2, 2)),
            dma((2, 3)),
        ],
        compiler_params=pltpu.CompilerParams(
            vmem_limit_bytes=60 * 1024 * 1024, collective_id=0, has_side_effects=True
        ),
    )(phases.reshape(-1), own_tiles, frames, masks[0][:, :, None, :], right, left, otf, apod)


def shards(frames, masks, phases, slot_tile, otf, apod):
    length = otf.shape[0]
    intersection = length - STRIDE
    own_tiles = slot_tile[0]

    return stitched_block(frames, masks, phases, own_tiles, otf, apod, intersection)


def solution(mesh):
    in_specs = (
        P("tx", "ty", None, None, None, None),
        P("tx", "ty", None, None),
        P("tx", "ty", None),
        P("tx", "ty"),
        P(),
        P(),
    )
    out_specs = P("ty", "tx")
    return jax.shard_map(shards, mesh=mesh, in_specs=in_specs, out_specs=out_specs, check_vma=False)
```
